1024 devices in a mesh: height: 128 (over x, z, core), cols: 8 (over y).
Axes of the slice: x: 4, y: 8, z: 16, core: 2. Of those that a mesh axis runs over, the one named last changes fastest.
Arguments:
- positions: float32 [3, 256, 64, 128], P(None, 'height', 'cols'), may hold values from -0.5 to 0.5
- velocities: float32 [3, 256, 64, 128], P(None, 'height', 'cols'), may hold values from -3 to 3
- contacts: int32 [9, 256, 64], P(None, 'height', 'cols'), may hold values 0 or 1
- exit_flags: int32 [256, 64], P('height', 'cols'), may hold values from 0 to 1, as said below
- inlet_slots: int32 [128, 64], P('height', 'cols'), may hold values from 0 to 7, as said below
- cell_blocks: int32 [256, 64], P('height', 'cols'), may hold values from 0 to 511
- cell_slots: int32 [256, 64, 128], P('height', 'cols'), may hold values from 0 to 127
- gas_source: float32 [256, 512, 512], P('height', 'cols'), may hold values from -12 to 12
- diagonal: float32 [256, 512, 512], P('height', 'cols'), may hold values from 0.25 to 2
Outputs:
- positions_out: float32 [3, 256, 64, 128], P(None, 'height', 'cols')
- velocities_out: float32 [3, 256, 64, 128], P(None, 'height', 'cols')
- pressure: float32 [256, 512, 512], P('height', 'cols')
- residual: float32 [256, 512, 512], P('height', 'cols')
The draws below stay inside these ranges and needn't reach their ends.
Inputs may be any that keep to these rules, and one draw needn't show every extreme that they name: `exit_flags`: only the top tile row of each device's 2 tile rows holds ones; at most 8 ones on one device, exactly 8 on some device. `inlet_slots`: each device's 8 entries are a permutation of 0 to 7.
All inputs are finite; a program needn't handle non-finite values. No bound on the sum of `contacts` on one device may be relied on, other than what follows from the above.
Results may differ from the reference program's by a relative error of at most 0.0003.
Values sent between devices are 32-bit elements; how exact they have to be, the bound alone decides.
A program may use at most 32 MiB of HBM per device.

```python
import jax
import jax.numpy as jnp
from jax import lax

P_SIZE = 128
TH = 2
TC = 8
GH = 2
GX = 64
GY = 512
ITERS = 2
SLABS = 128
COL_GROUPS = 8
TILE_ROWS = 256
TILE_COLS = 64
NZ = 256
NXC = 512
BLOCKS = 512


def draw_exit_flags(key, part):
    count_key, pick_key, order_key = jax.random.split(key, 3)
    counts = jax.random.randint(count_key, (SLABS, COL_GROUPS), 0, TC + 1)
    chosen = jax.random.randint(pick_key, (), 0, SLABS * COL_GROUPS)
    device_ids = jnp.arange(SLABS * COL_GROUPS, dtype=jnp.int32).reshape(SLABS, COL_GROUPS)
    counts = jnp.where(device_ids == chosen, TC, counts)
    scores = jax.random.randint(order_key, (SLABS, COL_GROUPS, TC), 0, 1 << 20) * TC + jnp.arange(TC, dtype=jnp.int32)
    ranks = jnp.argsort(jnp.argsort(scores, axis=-1), axis=-1)
    top_row = (ranks < counts[:, :, None]).astype(jnp.int32)
    whole = jnp.zeros((SLABS, TH, COL_GROUPS, TC), jnp.int32)
    whole = whole.at[:, TH - 1].set(top_row)
    return whole.reshape(SLABS * TH, COL_GROUPS * TC)


def draw_inlet_slots(key, part):
    scores = jax.random.randint(key, (SLABS, COL_GROUPS, TC), 0, 1 << 20) * TC + jnp.arange(TC, dtype=jnp.int32)
    order = jnp.argsort(scores, axis=-1).astype(jnp.int32)
    return order.reshape(SLABS, COL_GROUPS * TC)


def draw_gas_source(key, part):
    heights = jnp.arange(NZ, dtype=jnp.float32) / max(NZ - 1, 1)
    rising = (1.0 + 2.0 * heights)[:, None, None]
    rough = jnp.clip(jax.random.normal(key, (NZ, NXC, GY), jnp.float32), -4.0, 4.0)
    return rising * rough


def place_ends(result, stream_key, smallest, largest):
    longest = result.shape.index(max(result.shape))
    spots = []
    for shift in (0, 1):
        where = [jax.random.randint(jax.random.fold_in(stream_key, axis), (), 0, length) for axis, length in enumerate(result.shape)]
        where[longest] = (where[longest] + shift) % result.shape[longest]
        spots.append(tuple(where))
    return result.at[spots[0]].set(smallest).at[spots[1]].set(largest)


def shard_levels(own_key, extent, shards, low, largest):
    factor_of = 1.0
    for dim, blocks in shards:
        draws = jax.random.uniform(jax.random.fold_in(jax.random.fold_in(own_key, 6), dim), (blocks,), jnp.float32, low / len(shards), largest / len(shards))
        factor_of = factor_of * jnp.repeat(jnp.exp(draws), extent[dim] // blocks).reshape((-1,) + (1,) * (len(extent) - 1 - dim))
    return factor_of


def normal_values(rng, shape, scale, reach, cuts=(), kind=jnp.bfloat16):
    entries = scale * jax.random.normal(rng, shape, jnp.float32)
    if cuts:
        entries = entries * shard_levels(rng, shape, cuts, -0.22, 0.18)
    return jnp.clip(entries, -reach, reach).astype(kind)


def setup_inputs(seed: int = 0) -> dict:
    key_of = jax.random.split(jax.random.key(seed), 10)
    return {
        "positions": jnp.clip(jax.random.uniform(key_of[0], (3, TILE_ROWS, TILE_COLS, P_SIZE), jnp.float32, -0.5, 0.5) * shard_levels(key_of[0], (3, TILE_ROWS, TILE_COLS, P_SIZE), ((1, 128), (2, 8)), -0.4, 0.0), -0.5, 0.5),
        "velocities": normal_values(key_of[1], (3, TILE_ROWS, TILE_COLS, P_SIZE), 0.5, 3.0, ((1, 128), (2, 8)), jnp.float32),
        "contacts": place_ends((jax.random.randint(key_of[2], (9, TILE_ROWS, TILE_COLS), 0, 4) < 3).astype(jnp.int32), jax.random.fold_in(key_of[2], 1), 0, 1),
        "exit_flags": draw_exit_flags(jax.random.fold_in(key_of[9], 71), 0),
        "inlet_slots": draw_inlet_slots(jax.random.fold_in(key_of[9], 71), 0),
        "cell_blocks": place_ends(jax.random.randint(key_of[5], (TILE_ROWS, TILE_COLS), 0, BLOCKS), jax.random.fold_in(key_of[5], 1), 0, BLOCKS - 1).astype(jnp.int32),
        "cell_slots": place_ends(jax.random.randint(key_of[6], (TILE_ROWS, TILE_COLS, P_SIZE), 0, P_SIZE), jax.random.fold_in(key_of[6], 1), 0, P_SIZE - 1).astype(jnp.int32),
        "gas_source": draw_gas_source(jax.random.fold_in(key_of[9], 71), 0),
        "diagonal": jnp.clip(0.25 + 1.75 * jax.random.uniform(key_of[8], (NZ, NXC, GY), jnp.float32) ** shard_levels(key_of[8], (NZ, NXC, GY), ((0, 128), (1, 8)), -0.2, 0.2), 0.25, 2.0),
    }


spring = 0.05
cutoff_sq = 1.44
damping = 0.5
step_dt = 0.05
gravity = 1.0
deposit_gain = 2.0
highest = lax.Precision.HIGHEST


def row_forces(window, flags):
    width = flags.shape[1]
    centre = window[:, 1, 1:width + 1, :]
    places = centre[0:3]
    moving = places - damping * centre[3:6]
    own_sq = jnp.sum(places * places, axis=0)
    total = jnp.zeros(places.shape, jnp.float32)
    for row_step in range(3):
        for col_step in range(3):
            other = window[:, row_step, col_step:col_step + width, :]
            offset = jnp.array([col_step - 1.0, 0.0, row_step - 1.0], jnp.float32)[:, None, None]
            other_places = other[0:3] + offset
            cross = jnp.einsum("cip,ciq->ipq", places, other_places, precision=highest)
            other_sq = jnp.sum(other_places * other_places, axis=0)
            dist_sq = own_sq[:, :, None] + other_sq[:, None, :] - 2.0 * cross
            active = flags[row_step * 3 + col_step].astype(jnp.float32)
            weight = spring * jnp.maximum(1.0 - dist_sq / cutoff_sq, 0.0) * active[:, None, None]
            pulled = jnp.einsum("ipq,ciq->cip", weight, other_places - damping * other[3:6], precision=highest)
            total = total + moving * jnp.sum(weight, axis=2)[None] - pulled
    return total


def tile_forces(extended, flags):
    count = flags.shape[1]

    def one_row(index):
        window = lax.dynamic_slice_in_dim(extended, index, 3, 1)
        row_flags = lax.dynamic_slice_in_dim(flags, index, 1, 1)[:, 0]
        return row_forces(window, row_flags)

    stacked = lax.map(one_row, jnp.arange(count, dtype=jnp.int32))
    return jnp.transpose(stacked, (1, 0, 2, 3))


def advance(state, forces):
    upward = jnp.array([0.0, 0.0, 1.0], jnp.float32)[:, None, None, None]
    speeds = state[3:6] + step_dt * forces - step_dt * gravity * upward
    places = state[0:3] + step_dt * speeds
    return jnp.concatenate([places, speeds], axis=0)


def migrate(state, exit_flags, inlet_slots):
    chans, tile_rows, tile_cols, parts = state.shape
    slabs = tile_rows // TH
    groups = tile_cols // TC
    tiles = state.reshape(chans, slabs, TH, groups, TC, parts).transpose(0, 1, 3, 2, 4, 5)
    tiles = tiles.reshape(chans, slabs, groups, TH * TC, parts)
    leaving = exit_flags.reshape(slabs, TH, groups, TC).transpose(0, 2, 1, 3).reshape(slabs, groups, TH * TC)
    ranks = (jnp.cumsum(leaving, axis=2) - 1).astype(jnp.int32)
    buffer_ids = jnp.arange(TC, dtype=jnp.int32)
    picker = ((ranks[:, :, None, :] == buffer_ids[None, None, :, None]) & (leaving[:, :, None, :] > 0)).astype(jnp.float32)
    outgoing = jnp.einsum("sgkt,csgtp->csgkp", picker, tiles, precision=highest)
    kept = tiles * (1 - leaving).astype(jnp.float32)[None, :, :, :, None]
    arrived = jnp.roll(outgoing, 1, axis=1)
    targets = inlet_slots.reshape(slabs, groups, TC)
    placing = (targets[:, :, None, :] == buffer_ids[None, None, :, None]).astype(jnp.float32)
    bottom = jnp.einsum("sgjk,csgkp->csgjp", placing, arrived, precision=highest)
    tiles = jnp.concatenate([bottom, kept[:, :, :, TC:, :]], axis=3)
    tiles = tiles.reshape(chans, slabs, groups, TH, TC, parts).transpose(0, 1, 3, 2, 4, 5)
    return tiles.reshape(chans, tile_rows, tile_cols, parts)


def deposit(state, cell_blocks, cell_slots):
    chans, tile_rows, tile_cols, parts = state.shape
    slabs = tile_rows // TH
    groups = tile_cols // TC
    lifting = deposit_gain * state[5]
    blocks = GH * GX * GY // parts

    def one_slab(index):
        lifted = lax.dynamic_slice_in_dim(lifting, index * TH, TH, 0)
        slots = lax.dynamic_slice_in_dim(cell_slots, index * TH, TH, 0)
        owners = lax.dynamic_slice_in_dim(cell_blocks, index * TH, TH, 0)
        lifted = lifted.reshape(TH, groups, TC, parts).transpose(1, 0, 2, 3).reshape(groups, TH * TC, parts)
        slots = slots.reshape(TH, groups, TC, parts).transpose(1, 0, 2, 3).reshape(groups, TH * TC, parts)
        owners = owners.reshape(TH, groups, TC).transpose(1, 0, 2).reshape(groups, TH * TC)
        table = (slots[:, :, :, None] == jnp.arange(parts, dtype=jnp.int32)[None, None, None, :]).astype(jnp.float32)
        per_tile = jnp.einsum("gtp,gtpc->gtc", lifted, table, precision=highest)
        owner_table = (jnp.arange(blocks, dtype=jnp.int32)[None, :, None] == owners[:, None, :]).astype(jnp.float32)
        grid = jnp.einsum("gbt,gtc->gbc", owner_table, per_tile, precision=highest)
        return grid.reshape(groups, GH, GX, GY).transpose(1, 0, 2, 3).reshape(GH, groups * GX, GY)

    stacked = lax.map(one_slab, jnp.arange(slabs, dtype=jnp.int32))
    return stacked.reshape(slabs * GH, groups * GX, GY)


def operate(field, diagonal):
    padded = jnp.pad(field, 1)
    beside_all = padded[2:, 1:-1, 1:-1] + padded[:-2, 1:-1, 1:-1]
    beside_all = beside_all + padded[1:-1, 2:, 1:-1] + padded[1:-1, :-2, 1:-1]
    beside_all = beside_all + padded[1:-1, 1:-1, 2:] + padded[1:-1, 1:-1, :-2]
    return (6.0 + diagonal) * field - beside_all


def solve(right_side, diagonal):
    scaling = 1.0 / (6.0 + diagonal)
    solution = jnp.zeros_like(right_side)
    residual = right_side
    precond = residual * scaling
    weighted = jnp.sum(residual * precond)
    direction = precond
    for step in range(ITERS):
        image = operate(direction, diagonal)
        alpha = weighted / jnp.sum(direction * image)
        solution = solution + alpha * direction
        residual = residual - alpha * image
        if step + 1 < ITERS:
            precond = residual * scaling
            renewed = jnp.sum(residual * precond)
            direction = precond + (renewed / weighted) * direction
            weighted = renewed
    return solution, residual


def reference(positions, velocities, contacts, exit_flags, inlet_slots, cell_blocks, cell_slots, gas_source, diagonal):
    state = jnp.concatenate([positions, velocities], axis=0)
    for repeat in range(2):
        extended = jnp.pad(state, ((0, 0), (1, 1), (1, 1), (0, 0)))
        state = advance(state, tile_forces(extended, contacts))
    settled = state
    state = migrate(settled, exit_flags, inlet_slots)
    right_side = gas_source - deposit(settled, cell_blocks, cell_slots)
    solution, residual = solve(right_side, diagonal)
    return state[0:3], state[3:6], solution, residual
```

```python
import functools

import jax
import jax.numpy as jnp
from jax import lax
from jax.experimental import pallas as pl
from jax.experimental.pallas import tpu as pltpu
from jax.sharding import PartitionSpec as P

MESH = pl.DeviceIdType.MESH
F32 = jnp.float32
BF16 = jnp.bfloat16

spring = 0.05
cutoff_sq = 1.44
damping = 0.5
step_dt = 0.05
gravity = 1.0
deposit_gain = 2.0

PAD = 16
NT_DIMS = (((1,), (1,)), ((), ()))
TN_DIMS = (((0,), (0,)), ((), ()))


def split3(value):
    high = value.astype(BF16).astype(F32)
    rest = value - high
    mid = rest.astype(BF16).astype(F32)
    return high, mid, (rest - mid).astype(BF16).astype(F32)


def kernel(
    depth_z,
    pos_ref,
    vel_ref,
    slots_ref,
    contacts_ref,
    exit_ref,
    inlet_ref,
    blocks_ref,
    gas_ref,
    diag_ref,
    pos_out,
    vel_out,
    press_out,
    resid_out,
    tiles_a,
    tiles_b,
    grams,
    pulls,
    owns,
    total,
    settled,
    gas,
    scale,
    zed,
    image,
    weighed,
    twice,
    per_tile,
    block_row,
    leaving,
    arrived,
    row_a,
    rows_a,
    row_b,
    rows_b,
    load_sem,
    send_a,
    recv_a,
    send_b,
    recv_b,
    send_gas,
    recv_gas,
    send_diag,
    recv_diag,
    send_blk,
    recv_blk,
    send_dep,
    recv_dep,
    send_mig,
    recv_mig,
    send_ra,
    recv_ra,
    send_rb,
    recv_rb,
):
    high = lax.axis_size("height")
    wide = lax.axis_size("cols")
    h = lax.axis_index("height")
    c = lax.axis_index("cols")
    up = lax.rem(h + 1, high)
    down = lax.rem(h + high - 1, high)
    right = lax.rem(c + 1, wide)
    left = lax.rem(c + wide - 1, wide)
    goes = (
        (up, c),
        (down, c),
        (h, right),
        (h, left),
        (up, right),
        (up, left),
        (down, right),
        (down, left),
    )
    core = lax.rem(h, 2)
    z = lax.rem(h // 2, depth_z)
    x = h // (2 * depth_z)
    plane = (high // depth_z) * wide
    place = (x * 2 + core) * wide + c

    def z_peer(k):
        return ((x * depth_z + lax.rem(z + k, depth_z)) * 2 + core, c)

    def plane_peer(k):
        there = lax.rem(place + k, plane)
        pair = there // wide
        return (
            ((pair // 2) * depth_z + z) * 2 + lax.rem(pair, 2),
            lax.rem(there, wide),
        )

    own_rows = gas_ref.shape[1]
    first, last = PAD, PAD + own_rows
    own_span = pl.ds(first, own_rows)
    load_gas = pltpu.make_async_copy(
        gas_ref, gas.at[pl.ds(2, 2), own_span], load_sem.at[0]
    )
    load_diag = pltpu.make_async_copy(
        diag_ref, scale.at[pl.ds(2, 2), own_span], load_sem.at[1]
    )
    load_gas.start()
    load_diag.start()

    barrier = pltpu.get_barrier_semaphore()
    for target in goes:
        pl.semaphore_signal(barrier, inc=1, device_id=target, device_id_type=MESH)

    def greet_z(k, carry):
        pl.semaphore_signal(barrier, inc=1, device_id=z_peer(k), device_id_type=MESH)
        return carry

    def greet_plane(k, carry):
        pl.semaphore_signal(
            barrier, inc=1, device_id=plane_peer(k), device_id_type=MESH
        )
        return carry

    lax.fori_loop(1, depth_z, greet_z, 0)
    lax.fori_loop(1, plane, greet_plane, 0)

    def send(source, dest, send_sem, recv_sem, k):
        copy = pltpu.make_async_remote_copy(
            src_ref=source,
            dst_ref=dest,
            send_sem=send_sem.at[k],
            recv_sem=recv_sem.at[k],
            device_id=goes[k],
            device_id_type=MESH,
        )
        copy.start()
        return copy

    def send_tiles(tiles, send_sem, recv_sem):
        pairs = (
            (tiles.at[2, pl.ds(1, 8)], tiles.at[0, pl.ds(1, 8)]),
            (tiles.at[1, pl.ds(1, 8)], tiles.at[3, pl.ds(1, 8)]),
            (tiles.at[pl.ds(1, 2), 8], tiles.at[pl.ds(1, 2), 0]),
            (tiles.at[pl.ds(1, 2), 1], tiles.at[pl.ds(1, 2), 9]),
            (tiles.at[2, 8], tiles.at[0, 0]),
            (tiles.at[2, 1], tiles.at[0, 9]),
            (tiles.at[1, 8], tiles.at[3, 0]),
            (tiles.at[1, 1], tiles.at[3, 9]),
        )
        return [
            send(source, dest, send_sem, recv_sem, k)
            for k, (source, dest) in enumerate(pairs)
        ]

    def send_planes(field, send_sem, recv_sem):
        top, bottom = pl.ds(last - 8, 8), pl.ds(first, 8)
        before, after = pl.ds(first - 8, 8), pl.ds(last, 8)
        mid = pl.ds(2, 2)
        pairs = (
            (field.at[mid, own_span], field.at[pl.ds(0, 2), own_span]),
            (field.at[mid, own_span], field.at[pl.ds(4, 2), own_span]),
            (field.at[mid, top], field.at[mid, before]),
            (field.at[mid, bottom], field.at[mid, after]),
            (field.at[3, top], field.at[1, before]),
            (field.at[3, bottom], field.at[1, after]),
            (field.at[2, top], field.at[4, before]),
            (field.at[2, bottom], field.at[4, after]),
        )
        return [
            send(source, dest, send_sem, recv_sem, k)
            for k, (source, dest) in enumerate(pairs)
        ]

    comp = lax.broadcasted_iota(jnp.int32, (8, 128), 0)
    lane = lax.broadcasted_iota(jnp.int32, (8, 128), 1)

    for row in range(2):
        for part, ref in enumerate((pos_ref, vel_ref)):
            for axis in range(3):
                value = ref[axis, row]
                for col in range(8):
                    tiles_a[row + 1, col + 1, pl.ds(3 * part + axis, 1), :] = value[
                        col : col + 1
                    ]
        for col in range(8):
            tiles_a[row + 1, col + 1, pl.ds(6, 2), :] = jnp.zeros((2, 128), F32)

    blocks_vec = jnp.full((8, 128), -1, jnp.int32)
    for tile in range(16):
        blocks_vec = jnp.where(
            (lane < 48) & (lax.rem(lane, 16) == tile),
            blocks_ref[tile // 8, tile % 8],
            blocks_vec,
        )
    block_row[8] = blocks_vec.astype(F32)

    span = (2.0 * spring / cutoff_sq) ** 0.5

    def features(tiles, row, col, edge):
        tile = tiles[row, col]
        if edge is not None:
            tile = jnp.where(edge, tile, 0.0)
        shift_x = (col - 4.5) if isinstance(col, int) else (col.astype(F32) - 4.5)
        shift_z = (row - 1.5) if isinstance(row, int) else (row.astype(F32) - 1.5)
        shift = jnp.where(comp == 0, shift_x, jnp.where(comp == 2, shift_z, 0.0))
        at = tile + shift
        speed = pltpu.roll(tile, 5, 0)
        moving = at - damping * speed
        unit = jnp.where(comp < 3, span * at, 0.0)
        half = -0.5 * jnp.sum(unit * unit, axis=0, keepdims=True)
        gram = jnp.where(comp == 3, half, jnp.where(comp == 4, 1.0, unit))
        g_high, g_mid, g_low = split3(gram)
        lanes = pl.ds(col * 128, 128)
        if not isinstance(col, int):
            lanes = pl.ds(pl.multiple_of(col * 128, 128), 128)
        grams[row, :, lanes] = jnp.concatenate(
            [g_high, g_mid, g_high, g_mid, g_low, g_high], axis=0
        ).astype(BF16)
        pull = jnp.where(comp < 3, moving, jnp.where(comp == 3, 1.0, 0.0))
        p_high, p_mid, p_low = split3(pull)
        pulls[row, :, lanes] = jnp.concatenate(
            [jnp.where(comp < 4, p_high, pltpu.roll(p_low, 4, 0)), p_mid], axis=0
        ).astype(BF16)
        return unit, half

    def own_features(tiles, row, col):
        unit, half = features(tiles, row + 1, col + 1, None)
        gram = jnp.where(comp == 4, half + spring, jnp.where(comp == 3, 1.0, unit))
        f_high, f_mid, f_low = split3(gram)
        block = jnp.concatenate([f_high, f_high, f_mid, f_mid, f_high, f_low], axis=0)
        owns[row * 8 + col] = jnp.transpose(
            jnp.concatenate([block, jnp.zeros((80, 128), F32)], axis=0)
        )[:, :48].astype(BF16)
        total[row * 8 + col] = jnp.zeros((16, 128), F32)

    def interact(row, col, other):
        lanes = pl.ds(pl.multiple_of(col * 128, 128), 384)
        score = jnp.dot(
            owns[row * 8 + col], grams[other, :, lanes], preferred_element_type=F32
        )
        weight = jnp.maximum(score, 0.0)
        w_high = weight.astype(BF16)
        w_low = (weight - w_high.astype(F32)).astype(BF16)
        pull = pulls[other, :, lanes]
        kept = []
        for step in range(3):
            flag = contacts_ref[(other - row) * 3 + step, row, col].astype(F32)
            kept.append(
                pull[:, step * 128 : (step + 1) * 128]
                * jnp.full((16, 128), flag, F32).astype(BF16)
            )
        pull = jnp.concatenate(kept, axis=1)
        return lax.dot_general(
            pull, w_high, NT_DIMS, preferred_element_type=F32
        ) + lax.dot_general(pull, w_low, NT_DIMS, preferred_element_type=F32)

    def gather(row, col, others):
        result = interact(row, col, others[0])
        for other in others[1:]:
            result = result + interact(row, col, other)
        total[row * 8 + col] = total[row * 8 + col] + result

    def near(tiles):
        def make(index, carry):
            own_features(tiles, 0, index)
            own_features(tiles, 1, index)
            return carry

        lax.fori_loop(0, 8, make, 0)

        def inner(col, carry):
            gather(0, col, (1, 2))
            gather(1, col, (1, 2))
            return carry

        lax.fori_loop(1, 7, inner, 0)

    has_up, has_down = h < high - 1, h > 0
    has_right, has_left = c < wide - 1, c > 0

    def far(tiles):
        def beside(row, carry):
            features(tiles, row, 0, has_left)
            features(tiles, row, 9, has_right)
            return carry

        lax.fori_loop(1, 3, beside, 0)
        features(tiles, 0, 0, has_left & has_down)
        features(tiles, 0, 9, has_right & has_down)
        features(tiles, 3, 0, has_left & has_up)
        features(tiles, 3, 9, has_right & has_up)

        def above(col, carry):
            features(tiles, 0, col, has_down)
            features(tiles, 3, col, has_up)
            return carry

        lax.fori_loop(1, 9, above, 0)

        def inner(col, carry):
            gather(0, col, (0,))
            gather(1, col, (3,))
            return carry

        lax.fori_loop(1, 7, inner, 0)

        def outer(side, carry):
            gather(0, side * 7, (0, 1, 2))
            gather(1, side * 7, (1, 2, 3))
            return carry

        lax.fori_loop(0, 2, outer, 0)

    def advanced(tiles, row, col):
        tile = tiles[row + 1, col + 1]
        sums = total[row * 8 + col]
        front = sums[0:8]
        pulled = front + pltpu.roll(front, 4, 0) + sums[8:16]
        weight = front[3:4]
        shift = jnp.where(
            comp == 0,
            col.astype(F32) - 3.5,
            jnp.where(comp == 2, row - 0.5, 0.0),
        )
        moving = tile + shift - damping * pltpu.roll(tile, 5, 0)
        force = pltpu.roll(moving * weight - pulled, 3, 0)
        speeds = tile + step_dt * force - jnp.where(comp == 5, step_dt * gravity, 0.0)
        places = tile + step_dt * pltpu.roll(speeds, 5, 0)
        return jnp.where(comp < 3, places, jnp.where(comp < 6, speeds, 0.0))

    load_gas.wait()
    load_diag.wait()
    near(tiles_a)

    pl.semaphore_wait(barrier, 8 + (depth_z - 1) + (plane - 1))

    halo_a = send_tiles(tiles_a, send_a, recv_a)
    halo_gas = send_planes(gas, send_gas, recv_gas)
    halo_blk = [
        send(block_row.at[8], block_row.at[k], send_blk, recv_blk, k) for k in range(8)
    ]
    for copy in halo_a:
        copy.wait_recv()
    far(tiles_a)

    def first_step(col, carry):
        tiles_b[1, col + 1] = advanced(tiles_a, 0, col)
        tiles_b[2, col + 1] = advanced(tiles_a, 1, col)
        return carry

    lax.fori_loop(0, 8, first_step, 0)
    halo_b = send_tiles(tiles_b, send_b, recv_b)
    halo_diag = send_planes(scale, send_diag, recv_diag)
    near(tiles_b)
    for copy in halo_b:
        copy.wait_recv()
    far(tiles_b)

    count_row = lax.broadcasted_iota(jnp.int32, (128, 128), 0)

    def second_step(col, carry):
        for row in range(2):
            tile = advanced(tiles_b, row, col)
            settled[row * 8 + col] = tile
            lift = deposit_gain * tile[5:6]
            l_high, l_mid, l_low = split3(lift)
            rows = jnp.where(
                comp == 0,
                l_high,
                jnp.where(comp == 1, l_mid, jnp.where(comp == 2, l_low, 0.0)),
            )
            slot = slots_ref[row, pl.ds(col, 1), :]
            table = jnp.where(count_row == slot, 1.0, 0.0).astype(BF16)
            placed = lax.dot_general(
                jnp.concatenate([rows, jnp.zeros((8, 128), F32)], axis=0).astype(BF16),
                table,
                NT_DIMS,
                preferred_element_type=F32,
            )
            per_tile[8, pl.ds(row * 8 + col, 1), :] = jnp.sum(
                placed[0:8], axis=0, keepdims=True
            )
        return carry

    lax.fori_loop(0, 8, second_step, 0)
    halo_dep = [
        send(per_tile.at[8], per_tile.at[k], send_dep, recv_dep, k) for k in range(8)
    ]

    rank = jnp.int32(0)
    picks = [[None] * 8 for _ in range(8)]
    stays = []
    for col in range(8):
        flag = exit_ref[1, col]
        for k in range(8):
            picks[k][col] = jnp.where(rank == k, flag, 0).astype(F32)
        stays.append((1 - flag).astype(F32))
        rank = rank + flag
    for k in range(8):
        value = picks[k][0] * settled[8]
        for col in range(1, 8):
            value = value + picks[k][col] * settled[8 + col]
        leaving[k] = value
    move = pltpu.make_async_remote_copy(
        src_ref=leaving,
        dst_ref=arrived,
        send_sem=send_mig.at[0],
        recv_sem=recv_mig.at[0],
        device_id=(up, c),
        device_id_type=MESH,
    )
    move.start()

    for copy in halo_gas:
        copy.wait_recv()
    for copy in halo_diag:
        copy.wait_recv()
    for copy in halo_gas:
        copy.wait_send()
    for copy in halo_diag:
        copy.wait_send()
    for copy in halo_blk:
        copy.wait_recv()

    def enter(source, place_p, place_r, from_p, from_r, rows, valid):
        parts = jnp.concatenate(
            list(split3(per_tile[source])) + [jnp.zeros((80, 128), F32)], axis=0
        ).astype(BF16)
        owners = block_row[source][0:1]
        base = lax.broadcasted_iota(jnp.int32, (rows, 128), 0)
        for quarter in range(4):
            number = ((base + (from_p * own_rows + from_r)) * 4 + quarter).astype(F32)
            table = jnp.where(number == owners, 1.0, 0.0).astype(BF16)
            lanes = slice(quarter * 128, (quarter + 1) * 128)
            r0 = gas[place_p, place_r : place_r + rows, lanes] - jnp.dot(
                table, parts, preferred_element_type=F32
            )
            m = 1.0 / (6.0 + scale[place_p, place_r : place_r + rows, lanes])
            if valid is not None:
                m = jnp.where(valid, m, 0.0)
            gas[place_p, place_r : place_r + rows, lanes] = r0
            scale[place_p, place_r : place_r + rows, lanes] = m
            zed[place_p, place_r : place_r + rows, lanes] = m * r0

    far_row = own_rows - 8
    enter(8, 2, first, 0, 0, own_rows, None)
    enter(8, 3, first, 1, 0, own_rows, None)
    for copy in halo_dep:
        copy.wait_recv()
    enter(0, 0, first, 0, 0, own_rows, has_down)
    enter(0, 1, first, 1, 0, own_rows, has_down)
    enter(1, 4, first, 0, 0, own_rows, has_up)
    enter(1, 5, first, 1, 0, own_rows, has_up)
    for p in range(2):
        enter(2, 2 + p, first - 8, p, far_row, 8, has_left)
        enter(3, 2 + p, last, p, 0, 8, has_right)
    enter(4, 1, first - 8, 1, far_row, 8, has_left & has_down)
    enter(5, 1, last, 1, 0, 8, has_right & has_down)
    enter(6, 4, first - 8, 0, far_row, 8, has_left & has_up)
    enter(7, 4, last, 0, 0, 8, has_right & has_up)

    lane_w = lax.broadcasted_iota(jnp.int32, (8, 512), 1)

    def beside_sum(field, p, row):
        here = field[p, row : row + 8, :]
        ahead = jnp.where(lane_w == 0, 0.0, pltpu.roll(here, 1, 1))
        behind = jnp.where(lane_w == 511, 0.0, pltpu.roll(here, 511, 1))
        result = field[p + 1, row : row + 8, :] + field[p - 1, row : row + 8, :]
        result = result + field[p, row + 1 : row + 9, :]
        result = result + field[p, row - 1 : row + 7, :]
        return result + ahead + behind

    zero = jnp.zeros((8, 512), F32)
    dots = [zero, zero, zero, zero]
    for p in (2, 3, 1, 4):
        inside = p in (2, 3)
        start, stop = (first - 8, last + 8) if inside else (first, last)
        for row in range(start, stop, 8):
            r0 = gas[p, row : row + 8, :]
            u = r0 - beside_sum(zed, p, row)
            w = scale[p, row : row + 8, :] * u
            weighed[p, row : row + 8, :] = w
            if inside and first <= row < last:
                image[p, row : row + 8, :] = u
                z0 = zed[p, row : row + 8, :]
                dots[0] = dots[0] + r0 * z0
                dots[1] = dots[1] + z0 * u
                dots[2] = dots[2] + u * w
    for p in (2, 3):
        for row in range(first, last, 8):
            t = image[p, row : row + 8, :] - beside_sum(weighed, p, row)
            twice[p - 2, row - first : row - first + 8, :] = t
            dots[3] = dots[3] + weighed[p, row : row + 8, :] * t

    lane_one = lax.broadcasted_iota(jnp.int32, (1, 128), 1)
    mine = jnp.zeros((1, 128), F32)
    for k, dot in enumerate(dots):
        mine = jnp.where(lane_one == k, jnp.sum(dot), mine)
    row_a[0] = mine

    def reduce_over(count, peer, source, slots, send_sem, recv_sem):
        def begin(k, carry):
            pltpu.make_async_remote_copy(
                src_ref=source.at[0],
                dst_ref=slots.at[k - 1],
                send_sem=send_sem.at[k - 1],
                recv_sem=recv_sem.at[k - 1],
                device_id=peer(k),
                device_id_type=MESH,
            ).start()
            return carry

        lax.fori_loop(1, count, begin, 0)

        def end(k, carry):
            pltpu.make_async_remote_copy(
                src_ref=source.at[0],
                dst_ref=slots.at[k - 1],
                send_sem=send_sem.at[k - 1],
                recv_sem=recv_sem.at[k - 1],
                device_id=peer(k),
                device_id_type=MESH,
            ).wait()
            return carry

        return end

    end_a = reduce_over(depth_z, z_peer, row_a, rows_a, send_ra, recv_ra)

    move.wait()
    targets = [inlet_ref[0, k] for k in range(8)]
    for col in range(8):
        value = jnp.where(targets[0] == col, 1.0, 0.0) * arrived[0]
        for k in range(1, 8):
            value = value + jnp.where(targets[k] == col, 1.0, 0.0) * arrived[k]
        settled[col] = value
        settled[8 + col] = settled[8 + col] * stays[col]
    for row in range(2):
        for part, ref in enumerate((pos_out, vel_out)):
            for axis in range(3):
                for col in range(8):
                    ref[axis, row, pl.ds(col, 1), :] = settled[
                        row * 8 + col, pl.ds(3 * part + axis, 1), :
                    ]

    lax.fori_loop(1, depth_z, end_a, 0)
    mine = mine + jnp.sum(rows_a[...], axis=0)
    row_b[0] = mine
    end_b = reduce_over(plane, plane_peer, row_b, rows_b, send_rb, recv_rb)
    lax.fori_loop(1, plane, end_b, 0)
    mine = mine + jnp.sum(rows_b[...], axis=0)

    rz, energy, cross, third = (
        jnp.sum(jnp.where(lane_one == k, mine, 0.0), axis=1, keepdims=True)
        for k in range(4)
    )
    alpha = rz / energy
    renewed = alpha * alpha * cross - rz
    grow = 1.0 + renewed / rz
    second = renewed / (
        grow * grow * energy - 2.0 * grow * alpha * cross + alpha * alpha * third
    )
    near_factor = jnp.broadcast_to(alpha + second * grow, (8, 128))[:, 0:1]
    far_factor = jnp.broadcast_to(second * alpha, (8, 128))[:, 0:1]
    for p in range(2):
        for row in range(0, own_rows, 8):
            rows = slice(first + row, first + row + 8)
            press_out[p, row : row + 8, :] = (
                near_factor * zed[p + 2, rows, :]
                - far_factor * weighed[p + 2, rows, :]
            )
            resid_out[p, row : row + 8, :] = (
                gas[p + 2, rows, :]
                - near_factor * image[p + 2, rows, :]
                + far_factor * twice[p, row : row + 8, :]
            )

    for copy in halo_a + halo_b + halo_blk + halo_dep:
        copy.wait_send()


def on_device(
    depth_z,
    positions,
    velocities,
    contacts,
    exit_flags,
    inlet_slots,
    cell_blocks,
    cell_slots,
    gas_source,
    diagonal,
):
    high = lax.axis_size("height")
    plane = (high // depth_z) * lax.axis_size("cols")
    vmem = pl.BlockSpec(memory_space=pltpu.VMEM)
    smem = pl.BlockSpec(memory_space=pltpu.SMEM)
    hbm = pl.BlockSpec(memory_space=pl.ANY)
    dma = pltpu.SemaphoreType.DMA
    own_rows = gas_source.shape[1]
    grid = (6, own_rows + 2 * PAD, gas_source.shape[2])
    return pl.pallas_call(
        functools.partial(kernel, depth_z),
        out_shape=(
            jax.ShapeDtypeStruct(positions.shape, F32),
            jax.ShapeDtypeStruct(velocities.shape, F32),
            jax.ShapeDtypeStruct(gas_source.shape, F32),
            jax.ShapeDtypeStruct(gas_source.shape, F32),
        ),
        in_specs=[vmem, vmem, vmem, smem, smem, smem, smem, hbm, hbm],
        out_specs=(vmem, vmem, vmem, vmem),
        scratch_shapes=[
            pltpu.VMEM((4, 10, 8, 128), F32),
            pltpu.VMEM((4, 10, 8, 128), F32),
            pltpu.VMEM((4, 48, 1280), BF16),
            pltpu.VMEM((4, 16, 1280), BF16),
            pltpu.VMEM((16, 128, 48), BF16),
            pltpu.VMEM((16, 16, 128), F32),
            pltpu.VMEM((16, 8, 128), F32),
            pltpu.VMEM(grid, F32),
            pltpu.VMEM(grid, F32),
            pltpu.VMEM(grid, F32),
            pltpu.VMEM(grid, F32),
            pltpu.VMEM(grid, F32),
            pltpu.VMEM(gas_source.shape, F32),
            pltpu.VMEM((9, 16, 128), F32),
            pltpu.VMEM((9, 8, 128), F32),
            pltpu.VMEM((8, 8, 128), F32),
            pltpu.VMEM((8, 8, 128), F32),
            pltpu.VMEM((1, 1, 128), F32),
            pltpu.VMEM((depth_z - 1, 1, 128), F32),
            pltpu.VMEM((1, 1, 128), F32),
            pltpu.VMEM((plane - 1, 1, 128), F32),
            dma((2,)),
            dma((8,)),
            dma((8,)),
            dma((8,)),
            dma((8,)),
            dma((8,)),
            dma((8,)),
            dma((8,)),
            dma((8,)),
            dma((8,)),
            dma((8,)),
            dma((8,)),
            dma((8,)),
            dma((1,)),
            dma((1,)),
            dma((depth_z - 1,)),
            dma((depth_z - 1,)),
            dma((plane - 1,)),
            dma((plane - 1,)),
        ],
        compiler_params=pltpu.CompilerParams(
            collective_id=0, has_side_effects=True
        ),
    )(
        positions,
        velocities,
        cell_slots,
        contacts,
        exit_flags,
        inlet_slots,
        cell_blocks,
        gas_source,
        diagonal,
    )


def solution(mesh, depth_z=16):
    in_specs = (
        P(None, "height", "cols", None),
        P(None, "height", "cols", None),
        P(None, "height", "cols"),
        P("height", "cols"),
        P("height", "cols"),
        P("height", "cols"),
        P("height", "cols", None),
        P("height", "cols", None),
        P("height", "cols", None),
    )
    out_specs = (
        P(None, "height", "cols", None),
        P(None, "height", "cols", None),
        P("height", "cols", None),
        P("height", "cols", None),
    )
    return jax.shard_map(
        functools.partial(on_device, depth_z),
        mesh=mesh,
        in_specs=in_specs,
        out_specs=out_specs,
        check_vma=False,
    )
```

```python
import functools

import jax
import jax.numpy as jnp
from jax import lax
from jax.experimental import pallas as pl
from jax.experimental.pallas import tpu as pltpu
from jax.sharding import PartitionSpec as P

MESH = pl.DeviceIdType.MESH
F32 = jnp.float32
BF16 = jnp.bfloat16

spring = 0.05
cutoff_sq = 1.44
damping = 0.5
step_dt = 0.05
gravity = 1.0
deposit_gain = 2.0

PAD = 16
NT_DIMS = (((1,), (1,)), ((), ()))
TN_DIMS = (((0,), (0,)), ((), ()))


def split3(value):
    high = value.astype(BF16).astype(F32)
    rest = value - high
    mid = rest.astype(BF16).astype(F32)
    return high, mid, (rest - mid).astype(BF16).astype(F32)


def kernel(
    depth_z,
    pos_ref,
    vel_ref,
    slots_ref,
    contacts_ref,
    exit_ref,
    inlet_ref,
    blocks_ref,
    gas_ref,
    diag_ref,
    pos_out,
    vel_out,
    right_out,
    image_out,
    twice_out,
    sums_out,
    pos_buf,
    vel_buf,
    tiles_a,
    tiles_b,
    grams,
    pulls,
    owns,
    total,
    settled,
    gas,
    scale,
    zed,
    image,
    weighed,
    twice,
    per_tile,
    block_row,
    leaving,
    arrived,
    row_a,
    rows_a,
    row_b,
    rows_b,
    load_sem,
    store_sem,
    known_z,
    known_p,
    send_a,
    recv_a,
    send_b,
    recv_b,
    send_gas,
    recv_gas,
    send_diag,
    recv_diag,
    send_blk,
    recv_blk,
    send_dep,
    recv_dep,
    send_mig,
    recv_mig,
    send_ra,
    recv_ra,
    send_rb,
    recv_rb,
):
    high = lax.axis_size("height")
    wide = lax.axis_size("cols")
    h = lax.axis_index("height")
    c = lax.axis_index("cols")
    up = lax.rem(h + 1, high)
    down = lax.rem(h + high - 1, high)
    right = lax.rem(c + 1, wide)
    left = lax.rem(c + wide - 1, wide)
    goes = (
        (up, c),
        (down, c),
        (h, right),
        (h, left),
        (up, right),
        (up, left),
        (down, right),
        (down, left),
    )
    core = lax.rem(h, 2)
    z = lax.rem(h // 2, depth_z)
    x = h // (2 * depth_z)
    depth_x = high // (2 * depth_z)

    def z_peer(step):
        return (x * depth_z + lax.rem(z + step, depth_z)) * 2 + core

    def x_peer(step):
        return (lax.rem(x + step, depth_x) * depth_z + z) * 2 + core

    def y_peer(step):
        return lax.rem(c + step, wide)

    def far_first(steps, count):
        return sorted(steps, key=lambda step: -min(step, count - step))

    line_z = [z_peer(step) if step else h for step in range(depth_z)]
    line_x = [x_peer(step) if step else h for step in range(depth_x)]
    line_y = [y_peer(step) if step else c for step in range(wide)]
    other_core = 1 - 2 * core
    peers_a = [
        (line_z[step] + flip * other_core, c)
        for step in far_first(range(depth_z), depth_z)
        for flip in range(2)
        if step or flip
    ]
    peers_b = [
        (line_x[step_x], line_y[step_y])
        for step_y in far_first(range(wide), wide)
        for step_x in far_first(range(depth_x), depth_x)
        if step_x or step_y
    ]

    def signal(sem, target):
        pl.semaphore_signal(sem, inc=1, device_id=target, device_id_type=MESH)

    chain_z, chain_p = [], []
    reach = 1
    while reach < depth_z // 2:
        chain_z.append(((z_peer(reach), c), (z_peer(depth_z - reach), c)))
        reach *= 2
    chain_z.append(((h + other_core, c),))
    reach = 1
    while reach < wide // 2:
        chain_p.append(((h, y_peer(reach)), (h, y_peer(wide - reach))))
        reach *= 2
    for _ in range(depth_x // 2):
        chain_p.append(((x_peer(1), c), (x_peer(depth_x - 1), c)))
    stage = [0]

    def spread():
        now = stage[0]
        for chain, sem in ((chain_z, known_z), (chain_p, known_p)):
            if 0 < now <= len(chain):
                pl.semaphore_wait(sem.at[now - 1], len(chain[now - 1]))
        for chain, sem in ((chain_z, known_z), (chain_p, known_p)):
            if now < len(chain):
                for target in chain[now]:
                    signal(sem.at[now], target)
        stage[0] = now + 1

    own_rows = gas_ref.shape[1]
    first, last = PAD, PAD + own_rows
    own_span = pl.ds(first, own_rows)
    load_gas = pltpu.make_async_copy(
        gas_ref, gas.at[pl.ds(2, 2), own_span], load_sem.at[0]
    )
    load_diag = pltpu.make_async_copy(
        diag_ref, scale.at[pl.ds(2, 2), own_span], load_sem.at[1]
    )
    load_gas.start()
    load_diag.start()

    barrier = pltpu.get_barrier_semaphore()
    greeted = goes + (
        (z_peer(1), c),
        (z_peer(depth_z - 1), c),
        (x_peer(1), c),
        (x_peer(depth_x - 1), c),
    )
    for target in greeted:
        signal(barrier, target)

    def send(source, dest, send_sem, recv_sem, k):
        copy = pltpu.make_async_remote_copy(
            src_ref=source,
            dst_ref=dest,
            send_sem=send_sem.at[k],
            recv_sem=recv_sem.at[k],
            device_id=goes[k],
            device_id_type=MESH,
        )
        copy.start()
        return copy

    def send_tiles(tiles, send_sem, recv_sem):
        pairs = (
            (tiles.at[2, pl.ds(1, 8)], tiles.at[0, pl.ds(1, 8)]),
            (tiles.at[1, pl.ds(1, 8)], tiles.at[3, pl.ds(1, 8)]),
            (tiles.at[pl.ds(1, 2), 8], tiles.at[pl.ds(1, 2), 0]),
            (tiles.at[pl.ds(1, 2), 1], tiles.at[pl.ds(1, 2), 9]),
            (tiles.at[2, 8], tiles.at[0, 0]),
            (tiles.at[2, 1], tiles.at[0, 9]),
            (tiles.at[1, 8], tiles.at[3, 0]),
            (tiles.at[1, 1], tiles.at[3, 9]),
        )
        return [
            send(source, dest, send_sem, recv_sem, k)
            for k, (source, dest) in enumerate(pairs)
        ]

    def send_planes(field, send_sem, recv_sem):
        top, bottom = pl.ds(last - 8, 8), pl.ds(first, 8)
        before, after = pl.ds(first - 8, 8), pl.ds(last, 8)
        mid = pl.ds(2, 2)
        pairs = (
            (field.at[mid, own_span], field.at[pl.ds(0, 2), own_span]),
            (field.at[mid, own_span], field.at[pl.ds(4, 2), own_span]),
            (field.at[mid, top], field.at[mid, before]),
            (field.at[mid, bottom], field.at[mid, after]),
            (field.at[3, top], field.at[1, before]),
            (field.at[3, bottom], field.at[1, after]),
            (field.at[2, top], field.at[4, before]),
            (field.at[2, bottom], field.at[4, after]),
        )
        return [
            send(source, dest, send_sem, recv_sem, k)
            for k, (source, dest) in enumerate(pairs)
        ]

    comp = lax.broadcasted_iota(jnp.int32, (8, 128), 0)
    lane = lax.broadcasted_iota(jnp.int32, (8, 128), 1)

    for row in range(2):
        for part, ref in enumerate((pos_ref, vel_ref)):
            for axis in range(3):
                value = ref[axis, row]
                for col in range(8):
                    tiles_a[row + 1, col + 1, pl.ds(3 * part + axis, 1), :] = value[
                        col : col + 1
                    ]
        for col in range(8):
            tiles_a[row + 1, col + 1, pl.ds(6, 2), :] = jnp.zeros((2, 128), F32)

    blocks_vec = jnp.full((8, 128), -1, jnp.int32)
    for tile in range(16):
        blocks_vec = jnp.where(
            (lane < 48) & (lax.rem(lane, 16) == tile),
            blocks_ref[tile // 8, tile % 8],
            blocks_vec,
        )
    block_row[8] = blocks_vec.astype(F32)

    span = (2.0 * spring / cutoff_sq) ** 0.5

    def features(tiles, row, col, edge):
        tile = tiles[row, col]
        if edge is not None:
            tile = jnp.where(edge, tile, 0.0)
        shift_x = (col - 4.5) if isinstance(col, int) else (col.astype(F32) - 4.5)
        shift_z = (row - 1.5) if isinstance(row, int) else (row.astype(F32) - 1.5)
        shift = jnp.where(comp == 0, shift_x, jnp.where(comp == 2, shift_z, 0.0))
        at = tile + shift
        speed = pltpu.roll(tile, 5, 0)
        moving = at - damping * speed
        unit = jnp.where(comp < 3, span * at, 0.0)
        half = -0.5 * jnp.sum(unit * unit, axis=0, keepdims=True)
        gram = jnp.where(comp == 3, half, jnp.where(comp == 4, 1.0, unit))
        g_high, g_mid, g_low = split3(gram)
        lanes = pl.ds(col * 128, 128)
        if not isinstance(col, int):
            lanes = pl.ds(pl.multiple_of(col * 128, 128), 128)
        grams[row, :, lanes] = jnp.concatenate(
            [g_high, g_mid, g_high, g_mid, g_low, g_high], axis=0
        ).astype(BF16)
        pull = jnp.where(comp < 3, moving, jnp.where(comp == 3, 1.0, 0.0))
        pull = jnp.where(comp < 4, pull, pltpu.roll(pull, 4, 0))
        products = [
            pull * jnp.where(comp < 4, unit[0:1], unit[1:2]),
            pull * jnp.where(comp < 4, unit[2:3], half),
            jnp.where(comp < 4, pull, 0.0),
        ]
        parts = [split3(product) for product in products]
        pulls[row, :, lanes] = jnp.concatenate(
            [part[level] for level in range(3) for part in parts]
            + [jnp.zeros((8, 128), F32)],
            axis=0,
        ).astype(BF16)
        return unit, half

    def own_features(tiles, row, col):
        unit, half = features(tiles, row + 1, col + 1, None)
        gram = jnp.where(comp == 4, half + spring, jnp.where(comp == 3, 1.0, unit))
        f_high, f_mid, f_low = split3(gram)
        block = jnp.concatenate([f_high, f_high, f_mid, f_mid, f_high, f_low], axis=0)
        owns[row * 8 + col] = jnp.transpose(
            jnp.concatenate([block, jnp.zeros((80, 128), F32)], axis=0)
        )[:, :48].astype(BF16)
        total[row * 8 + col] = jnp.zeros((24, 128), F32)

    def gather(row, col, pieces):
        spans = []
        for other, start, count in pieces:
            begin = (col + start) * 128
            if not isinstance(col, int):
                begin = pl.multiple_of(begin, 128)
            spans.append((other, pl.ds(begin, count * 128)))
        gram = jnp.concatenate([grams[other, :, lanes] for other, lanes in spans], 1)
        pull = jnp.concatenate([pulls[other, :, lanes] for other, lanes in spans], 1)
        score = jnp.dot(owns[row * 8 + col], gram, preferred_element_type=F32)
        kept = []
        for other, start, count in pieces:
            for step in range(start, start + count):
                flag = contacts_ref[row, col, (other - row) * 3 + step].astype(F32)
                here = score[:, len(kept) * 128 : (len(kept) + 1) * 128]
                kept.append(jnp.where(here > 0.0, flag, 0.0).astype(BF16))
        result = lax.dot_general(
            pull, jnp.concatenate(kept, 1), NT_DIMS, preferred_element_type=F32
        )
        total[row * 8 + col] = total[row * 8 + col] + (
            result[0:24] + result[24:48] + result[48:72]
        )

    def near(tiles):
        def make(index, carry):
            own_features(tiles, 0, index)
            own_features(tiles, 1, index)
            return carry

        lax.fori_loop(0, 8, make, 0)

        def inner(col, carry):
            gather(0, col, ((1, 0, 3), (2, 0, 3)))
            gather(1, col, ((1, 0, 3), (2, 0, 3)))
            return carry

        lax.fori_loop(1, 7, inner, 0)
        for row in range(2):
            gather(row, 0, ((1, 1, 2), (2, 1, 2)))
            gather(row, 7, ((1, 0, 2), (2, 0, 2)))

    has_up, has_down = h < high - 1, h > 0
    has_right, has_left = c < wide - 1, c > 0

    def far(tiles):
        def beside(row, carry):
            features(tiles, row, 0, has_left)
            features(tiles, row, 9, has_right)
            return carry

        lax.fori_loop(1, 3, beside, 0)
        features(tiles, 0, 0, has_left & has_down)
        features(tiles, 0, 9, has_right & has_down)
        features(tiles, 3, 0, has_left & has_up)
        features(tiles, 3, 9, has_right & has_up)

        def above(col, carry):
            features(tiles, 0, col, has_down)
            features(tiles, 3, col, has_up)
            return carry

        lax.fori_loop(1, 9, above, 0)

        def inner(col, carry):
            gather(0, col, ((0, 0, 3),))
            gather(1, col, ((3, 0, 3),))
            return carry

        lax.fori_loop(1, 7, inner, 0)
        for row in range(2):
            gather(row, 0, ((3 * row, 0, 3), (1, 0, 1), (2, 0, 1)))
            gather(row, 7, ((3 * row, 0, 3), (1, 2, 1), (2, 2, 1)))

    def advanced(tiles, row, col):
        tile = tiles[row + 1, col + 1]
        sums = total[row * 8 + col]
        shift = jnp.where(
            comp == 0,
            col.astype(F32) - 3.5,
            jnp.where(comp == 2, row - 0.5, 0.0),
        )
        at = tile + shift
        moving = at - damping * pltpu.roll(tile, 5, 0)
        unit = jnp.where(comp < 3, span * at, 0.0)
        half = -0.5 * jnp.sum(unit * unit, axis=0, keepdims=True)
        pulled = (
            sums[0:8] * jnp.where(comp < 4, unit[0:1], unit[1:2])
            + sums[8:16] * jnp.where(comp < 4, unit[2:3], 1.0)
            + sums[16:24] * (half + spring)
        )
        pulled = pulled + pltpu.roll(pulled, 4, 0)
        force = pltpu.roll(moving * pulled[3:4] - pulled, 3, 0)
        speeds = tile + step_dt * force - jnp.where(comp == 5, step_dt * gravity, 0.0)
        places = tile + step_dt * pltpu.roll(speeds, 5, 0)
        return jnp.where(comp < 3, places, jnp.where(comp < 6, speeds, 0.0))

    load_gas.wait()
    load_diag.wait()
    near(tiles_a)

    pl.semaphore_wait(barrier, len(greeted))

    halo_a = send_tiles(tiles_a, send_a, recv_a)
    halo_gas = send_planes(gas, send_gas, recv_gas)
    halo_blk = [
        send(block_row.at[8], block_row.at[k], send_blk, recv_blk, k) for k in range(8)
    ]
    spread()
    for copy in halo_a:
        copy.wait_recv()
    spread()
    far(tiles_a)
    spread()

    def first_step(col, carry):
        tiles_b[1, col + 1] = advanced(tiles_a, 0, col)
        tiles_b[2, col + 1] = advanced(tiles_a, 1, col)
        return carry

    lax.fori_loop(0, 8, first_step, 0)
    halo_b = send_tiles(tiles_b, send_b, recv_b)
    halo_diag = send_planes(scale, send_diag, recv_diag)
    near(tiles_b)
    spread()
    for copy in halo_b:
        copy.wait_recv()
    far(tiles_b)
    spread()

    count_row = lax.broadcasted_iota(jnp.int32, (128, 128), 0)

    def second_step(col, carry):
        for row in range(2):
            tile = advanced(tiles_b, row, col)
            settled[row * 8 + col] = tile
            lift = deposit_gain * tile[5:6]
            l_high, l_mid, l_low = split3(lift)
            rows = jnp.where(
                comp == 0,
                l_high,
                jnp.where(comp == 1, l_mid, jnp.where(comp == 2, l_low, 0.0)),
            )
            slot = slots_ref[row, pl.ds(col, 1), :]
            table = jnp.where(count_row == slot, 1.0, 0.0).astype(BF16)
            placed = lax.dot_general(
                jnp.concatenate([rows, jnp.zeros((8, 128), F32)], axis=0).astype(BF16),
                table,
                NT_DIMS,
                preferred_element_type=F32,
            )
            per_tile[8, pl.ds(row * 8 + col, 1), :] = jnp.sum(
                placed[0:8], axis=0, keepdims=True
            )
        return carry

    lax.fori_loop(0, 8, second_step, 0)
    halo_dep = [
        send(per_tile.at[8], per_tile.at[k], send_dep, recv_dep, k) for k in range(8)
    ]

    rank = jnp.int32(0)
    picks = [[None] * 8 for _ in range(8)]
    stays = []
    for col in range(8):
        flag = exit_ref[1, col]
        for k in range(8):
            picks[k][col] = jnp.where(rank == k, flag, 0).astype(F32)
        stays.append((1 - flag).astype(F32))
        rank = rank + flag
    for k in range(8):
        value = picks[k][0] * settled[8]
        for col in range(1, 8):
            value = value + picks[k][col] * settled[8 + col]
        leaving[k] = value
    move = pltpu.make_async_remote_copy(
        src_ref=leaving,
        dst_ref=arrived,
        send_sem=send_mig.at[0],
        recv_sem=recv_mig.at[0],
        device_id=(up, c),
        device_id_type=MESH,
    )
    move.start()

    for copy in halo_gas:
        copy.wait_recv()
    for copy in halo_diag:
        copy.wait_recv()
    for copy in halo_gas:
        copy.wait_send()
    for copy in halo_diag:
        copy.wait_send()
    for copy in halo_blk:
        copy.wait_recv()

    def enter(source, place_p, place_r, from_p, from_r, rows, valid):
        parts = jnp.concatenate(
            list(split3(per_tile[source])) + [jnp.zeros((80, 128), F32)], axis=0
        ).astype(BF16)
        owners = block_row[source][0:1]
        base = lax.broadcasted_iota(jnp.int32, (rows, 128), 0)
        for quarter in range(4):
            number = ((base + (from_p * own_rows + from_r)) * 4 + quarter).astype(F32)
            table = jnp.where(number == owners, 1.0, 0.0).astype(BF16)
            lanes = slice(quarter * 128, (quarter + 1) * 128)
            r0 = gas[place_p, place_r : place_r + rows, lanes] - jnp.dot(
                table, parts, preferred_element_type=F32
            )
            m = 1.0 / (6.0 + scale[place_p, place_r : place_r + rows, lanes])
            if valid is not None:
                m = jnp.where(valid, m, 0.0)
            gas[place_p, place_r : place_r + rows, lanes] = r0
            scale[place_p, place_r : place_r + rows, lanes] = m
            zed[place_p, place_r : place_r + rows, lanes] = m * r0

    far_row = own_rows - 8
    enter(8, 2, first, 0, 0, own_rows, None)
    enter(8, 3, first, 1, 0, own_rows, None)
    for copy in halo_dep:
        copy.wait_recv()
    enter(0, 0, first, 0, 0, own_rows, has_down)
    enter(0, 1, first, 1, 0, own_rows, has_down)
    enter(1, 4, first, 0, 0, own_rows, has_up)
    enter(1, 5, first, 1, 0, own_rows, has_up)
    for p in range(2):
        enter(2, 2 + p, first - 8, p, far_row, 8, has_left)
        enter(3, 2 + p, last, p, 0, 8, has_right)
    enter(4, 1, first - 8, 1, far_row, 8, has_left & has_down)
    enter(5, 1, last, 1, 0, 8, has_right & has_down)
    enter(6, 4, first - 8, 0, far_row, 8, has_left & has_up)
    enter(7, 4, last, 0, 0, 8, has_right & has_up)

    lane_w = lax.broadcasted_iota(jnp.int32, (8, 512), 1)

    def beside_sum(field, p, row):
        here = field[p, row : row + 8, :]
        ahead = jnp.where(lane_w == 0, 0.0, pltpu.roll(here, 1, 1))
        behind = jnp.where(lane_w == 511, 0.0, pltpu.roll(here, 511, 1))
        result = field[p + 1, row : row + 8, :] + field[p - 1, row : row + 8, :]
        result = result + field[p, row + 1 : row + 9, :]
        result = result + field[p, row - 1 : row + 7, :]
        return result + ahead + behind

    zero = jnp.zeros((8, 512), F32)
    dots = [zero, zero, zero, zero]
    for p in (2, 3, 1, 4):
        inside = p in (2, 3)
        start, stop = (first - 8, last + 8) if inside else (first, last)
        for row in range(start, stop, 8):
            r0 = gas[p, row : row + 8, :]
            u = r0 - beside_sum(zed, p, row)
            w = scale[p, row : row + 8, :] * u
            weighed[p, row : row + 8, :] = w
            if inside and first <= row < last:
                image[p, row : row + 8, :] = u
                z0 = zed[p, row : row + 8, :]
                dots[0] = dots[0] + r0 * z0
                dots[1] = dots[1] + z0 * u
                dots[2] = dots[2] + u * w
    for p in (2, 3):
        for row in range(first, last, 8):
            t = image[p, row : row + 8, :] - beside_sum(weighed, p, row)
            twice[p - 2, row - first : row - first + 8, :] = t
            dots[3] = dots[3] + weighed[p, row : row + 8, :] * t

    lane_one = lax.broadcasted_iota(jnp.int32, (1, 128), 1)
    mine = jnp.zeros((1, 128), F32)
    for k, dot in enumerate(dots):
        mine = jnp.where(lane_one == k, jnp.sum(dot), mine)
    row_a[0] = mine

    def share(peers, source, slots, send_sem, recv_sem):
        copies = []
        for k, target in enumerate(peers):
            copies.append(
                pltpu.make_async_remote_copy(
                    src_ref=source.at[0],
                    dst_ref=slots.at[k],
                    send_sem=send_sem.at[k],
                    recv_sem=recv_sem.at[k],
                    device_id=target,
                    device_id_type=MESH,
                )
            )
            copies[-1].start()
        return copies

    sums_a = share(peers_a, row_a, rows_a, send_ra, recv_ra)
    stores = [
        pltpu.make_async_copy(
            gas.at[pl.ds(2, 2), own_span], right_out, store_sem.at[0]
        ),
        pltpu.make_async_copy(
            image.at[pl.ds(2, 2), own_span], image_out, store_sem.at[1]
        ),
        pltpu.make_async_copy(twice, twice_out, store_sem.at[2]),
    ]
    for copy in stores:
        copy.start()

    move.wait()
    targets = [inlet_ref[0, k] for k in range(8)]
    for col in range(8):
        value = jnp.where(targets[0] == col, 1.0, 0.0) * arrived[0]
        for k in range(1, 8):
            value = value + jnp.where(targets[k] == col, 1.0, 0.0) * arrived[k]
        settled[col] = value
        settled[8 + col] = settled[8 + col] * stays[col]
    for row in range(2):
        for part, ref in enumerate((pos_buf, vel_buf)):
            for axis in range(3):
                for col in range(8):
                    ref[axis, row, pl.ds(col, 1), :] = settled[
                        row * 8 + col, pl.ds(3 * part + axis, 1), :
                    ]

    stores += [
        pltpu.make_async_copy(pos_buf, pos_out, store_sem.at[3]),
        pltpu.make_async_copy(vel_buf, vel_out, store_sem.at[4]),
    ]
    for copy in stores[3:]:
        copy.start()
    for copy in halo_a + halo_b + halo_blk + halo_dep:
        copy.wait_send()

    for copy in sums_a:
        copy.wait_recv()
    mine = mine + jnp.sum(rows_a[...], axis=0)
    row_b[0] = mine
    sums_b = share(peers_b, row_b, rows_b, send_rb, recv_rb)
    for copy in sums_a:
        copy.wait_send()
    for copy in stores:
        copy.wait()
    for copy in sums_b:
        copy.wait_recv()
    sums_out[...] = mine + jnp.sum(rows_b[...], axis=0)
    for copy in sums_b:
        copy.wait_send()


def finish(sums, right, image, twice, diag, pos, vel, pos_out, vel_out, press, resid):
    lane = lax.broadcasted_iota(jnp.int32, (1, 128), 1)
    rz, energy, cross, third = (
        jnp.sum(jnp.where(lane == k, sums[...], 0.0), axis=1, keepdims=True)
        for k in range(4)
    )
    alpha = rz / energy
    renewed = alpha * alpha * cross - rz
    grow = 1.0 + renewed / rz
    second = renewed / (
        grow * grow * energy - 2.0 * grow * alpha * cross + alpha * alpha * third
    )
    near_factor = jnp.broadcast_to(alpha + second * grow, (8, 128))[:, 0:1]
    far_factor = jnp.broadcast_to(second * alpha, (8, 128))[:, 0:1]
    for p in range(2):
        for row in range(0, right.shape[1], 8):
            rows = slice(row, row + 8)
            r0, u = right[p, rows, :], image[p, rows, :]
            m = 1.0 / (6.0 + diag[p, rows, :])
            press[p, rows, :] = m * (near_factor * r0 - far_factor * u)
            resid[p, rows, :] = r0 - near_factor * u + far_factor * twice[p, rows, :]
    pos_out[...] = pos[...]
    vel_out[...] = vel[...]


def on_device(
    depth_z,
    positions,
    velocities,
    contacts,
    exit_flags,
    inlet_slots,
    cell_blocks,
    cell_slots,
    gas_source,
    diagonal,
):
    high = lax.axis_size("height")
    count_a = 2 * depth_z - 1
    count_b = (high // (2 * depth_z)) * lax.axis_size("cols") - 1
    vmem = pl.BlockSpec(memory_space=pltpu.VMEM)
    smem = pl.BlockSpec(memory_space=pltpu.SMEM)
    hbm = pl.BlockSpec(memory_space=pl.ANY)
    dma = pltpu.SemaphoreType.DMA
    own_rows = gas_source.shape[1]
    grid = (6, own_rows + 2 * PAD, gas_source.shape[2])
    field = jax.ShapeDtypeStruct(gas_source.shape, F32)
    state = jax.ShapeDtypeStruct(positions.shape, F32)
    row = jax.ShapeDtypeStruct((1, 128), F32)
    pos, vel, right, image, twice, sums = pl.pallas_call(
        functools.partial(kernel, depth_z),
        out_shape=(state, state, field, field, field, row),
        in_specs=[vmem, vmem, vmem, smem, smem, smem, smem, hbm, hbm],
        out_specs=(hbm, hbm, hbm, hbm, hbm, vmem),
        scratch_shapes=[
            pltpu.VMEM(positions.shape, F32),
            pltpu.VMEM(positions.shape, F32),
            pltpu.VMEM((4, 10, 8, 128), F32),
            pltpu.VMEM((4, 10, 8, 128), F32),
            pltpu.VMEM((4, 48, 1280), BF16),
            pltpu.VMEM((4, 80, 1280), BF16),
            pltpu.VMEM((16, 128, 48), BF16),
            pltpu.VMEM((16, 24, 128), F32),
            pltpu.VMEM((16, 8, 128), F32),
            pltpu.VMEM(grid, F32),
            pltpu.VMEM(grid, F32),
            pltpu.VMEM(grid, F32),
            pltpu.VMEM(grid, F32),
            pltpu.VMEM(grid, F32),
            pltpu.VMEM(gas_source.shape, F32),
            pltpu.VMEM((9, 16, 128), F32),
            pltpu.VMEM((9, 8, 128), F32),
            pltpu.VMEM((8, 8, 128), F32),
            pltpu.VMEM((8, 8, 128), F32),
            pltpu.VMEM((1, 1, 128), F32),
            pltpu.VMEM((count_a, 1, 128), F32),
            pltpu.VMEM((1, 1, 128), F32),
            pltpu.VMEM((count_b, 1, 128), F32),
            dma((2,)),
            dma((5,)),
            pltpu.SemaphoreType.REGULAR((8,)),
            pltpu.SemaphoreType.REGULAR((8,)),
            dma((8,)),
            dma((8,)),
            dma((8,)),
            dma((8,)),
            dma((8,)),
            dma((8,)),
            dma((8,)),
            dma((8,)),
            dma((8,)),
            dma((8,)),
            dma((8,)),
            dma((8,)),
            dma((1,)),
            dma((1,)),
            dma((count_a,)),
            dma((count_a,)),
            dma((count_b,)),
            dma((count_b,)),
        ],
        compiler_params=pltpu.CompilerParams(
            collective_id=0, has_side_effects=True
        ),
    )(
        positions,
        velocities,
        cell_slots,
        jnp.transpose(contacts, (1, 2, 0)),
        exit_flags,
        inlet_slots,
        cell_blocks,
        gas_source,
        diagonal,
    )
    return pl.pallas_call(
        finish,
        out_shape=(state, state, field, field),
        in_specs=[vmem] * 7,
        out_specs=(vmem,) * 4,
    )(sums, right, image, twice, diagonal, pos, vel)


def solution(mesh, depth_z=16):
    in_specs = (
        P(None, "height", "cols", None),
        P(None, "height", "cols", None),
        P(None, "height", "cols"),
        P("height", "cols"),
        P("height", "cols"),
        P("height", "cols"),
        P("height", "cols", None),
        P("height", "cols", None),
        P("height", "cols", None),
    )
    out_specs = (
        P(None, "height", "cols", None),
        P(None, "height", "cols", None),
        P("height", "cols", None),
        P("height", "cols", None),
    )
    return jax.shard_map(
        functools.partial(on_device, depth_z),
        mesh=mesh,
        in_specs=in_specs,
        out_specs=out_specs,
        check_vma=False,
    )
```

```python
import functools

import jax
import jax.numpy as jnp
from jax import lax
from jax.experimental import pallas as pl
from jax.experimental.pallas import tpu as pltpu
from jax.sharding import PartitionSpec as P

MESH = pl.DeviceIdType.MESH
F32 = jnp.float32
BF16 = jnp.bfloat16

spring = 0.05
cutoff_sq = 1.44
damping = 0.5
step_dt = 0.05
gravity = 1.0
deposit_gain = 2.0

PAD = 16
NT_DIMS = (((1,), (1,)), ((), ()))
TN_DIMS = (((0,), (0,)), ((), ()))


def split3(value):
    high = value.astype(BF16).astype(F32)
    rest = value - high
    mid = rest.astype(BF16).astype(F32)
    return high, mid, (rest - mid).astype(BF16).astype(F32)


def kernel(
    depth_z,
    pos_ref,
    vel_ref,
    slots_ref,
    contacts_ref,
    exit_ref,
    inlet_ref,
    blocks_ref,
    gas_ref,
    diag_ref,
    pos_out,
    vel_out,
    right_out,
    image_out,
    twice_out,
    sums_out,
    pos_buf,
    vel_buf,
    tiles_a,
    tiles_b,
    grams,
    pulls,
    owns,
    total,
    settled,
    gas,
    scale,
    recip,
    zed,
    image,
    weighed,
    twice,
    per_tile,
    block_row,
    leaving,
    arrived,
    row_a,
    rows_a,
    row_b,
    rows_b,
    load_sem,
    store_sem,
    known_z,
    known_p,
    send_a,
    recv_a,
    send_b,
    recv_b,
    send_gas,
    recv_gas,
    send_diag,
    recv_diag,
    send_blk,
    recv_blk,
    send_dep,
    recv_dep,
    send_mig,
    recv_mig,
    send_ra,
    recv_ra,
    send_rb,
    recv_rb,
):
    high = lax.axis_size("height")
    wide = lax.axis_size("cols")
    h = lax.axis_index("height")
    c = lax.axis_index("cols")
    up = lax.rem(h + 1, high)
    down = lax.rem(h + high - 1, high)
    right = lax.rem(c + 1, wide)
    left = lax.rem(c + wide - 1, wide)
    goes = (
        (up, c),
        (down, c),
        (h, right),
        (h, left),
        (up, right),
        (up, left),
        (down, right),
        (down, left),
    )
    core = lax.rem(h, 2)
    z = lax.rem(h // 2, depth_z)
    x = h // (2 * depth_z)
    depth_x = high // (2 * depth_z)

    def z_peer(step):
        return (x * depth_z + lax.rem(z + step, depth_z)) * 2 + core

    def x_peer(step):
        return (lax.rem(x + step, depth_x) * depth_z + z) * 2 + core

    def y_peer(step):
        return lax.rem(c + step, wide)

    def far_first(steps, count):
        return sorted(steps, key=lambda step: -min(step, count - step))

    line_z = [z_peer(step) if step else h for step in range(depth_z)]
    line_x = [x_peer(step) if step else h for step in range(depth_x)]
    line_y = [y_peer(step) if step else c for step in range(wide)]
    other_core = 1 - 2 * core
    peers_a = [
        (line_z[step] + flip * other_core, c)
        for step in far_first(range(depth_z), depth_z)
        for flip in range(2)
        if step or flip
    ]
    peers_b = [
        (line_x[step_x], line_y[step_y])
        for step_y in far_first(range(wide), wide)
        for step_x in far_first(range(depth_x), depth_x)
        if step_x or step_y
    ]

    def signal(sem, target):
        pl.semaphore_signal(sem, inc=1, device_id=target, device_id_type=MESH)

    chain_z, chain_p = [], []
    reach = 1
    while reach < depth_z // 2:
        chain_z.append(((z_peer(reach), c), (z_peer(depth_z - reach), c)))
        reach *= 2
    chain_z.append(((h + other_core, c),))
    reach = 1
    while reach < wide // 2:
        chain_p.append(((h, y_peer(reach)), (h, y_peer(wide - reach))))
        reach *= 2
    for _ in range(depth_x // 2):
        chain_p.append(((x_peer(1), c), (x_peer(depth_x - 1), c)))
    stage = [0]

    def spread():
        now = stage[0]
        for chain, sem in ((chain_z, known_z), (chain_p, known_p)):
            if 0 < now <= len(chain):
                pl.semaphore_wait(sem.at[now - 1], len(chain[now - 1]))
        for chain, sem in ((chain_z, known_z), (chain_p, known_p)):
            if now < len(chain):
                for target in chain[now]:
                    signal(sem.at[now], target)
        stage[0] = now + 1

    own_rows = gas_ref.shape[1]
    first, last = PAD, PAD + own_rows
    own_span = pl.ds(first, own_rows)
    load_gas = pltpu.make_async_copy(
        gas_ref, gas.at[pl.ds(2, 2), own_span], load_sem.at[0]
    )
    load_diag = pltpu.make_async_copy(
        diag_ref, scale.at[pl.ds(2, 2), own_span], load_sem.at[1]
    )
    load_gas.start()
    load_diag.start()

    barrier = pltpu.get_barrier_semaphore()
    greeted = goes + (
        (z_peer(1), c),
        (z_peer(depth_z - 1), c),
        (x_peer(1), c),
        (x_peer(depth_x - 1), c),
    )
    for target in greeted:
        signal(barrier, target)

    def send(source, dest, send_sem, recv_sem, k):
        copy = pltpu.make_async_remote_copy(
            src_ref=source,
            dst_ref=dest,
            send_sem=send_sem.at[k],
            recv_sem=recv_sem.at[k],
            device_id=goes[k],
            device_id_type=MESH,
        )
        copy.start()
        return copy

    def send_tiles(tiles, send_sem, recv_sem):
        pairs = (
            (tiles.at[2, pl.ds(1, 8)], tiles.at[0, pl.ds(1, 8)]),
            (tiles.at[1, pl.ds(1, 8)], tiles.at[3, pl.ds(1, 8)]),
            (tiles.at[pl.ds(1, 2), 8], tiles.at[pl.ds(1, 2), 0]),
            (tiles.at[pl.ds(1, 2), 1], tiles.at[pl.ds(1, 2), 9]),
            (tiles.at[2, 8], tiles.at[0, 0]),
            (tiles.at[2, 1], tiles.at[0, 9]),
            (tiles.at[1, 8], tiles.at[3, 0]),
            (tiles.at[1, 1], tiles.at[3, 9]),
        )
        return [
            send(source, dest, send_sem, recv_sem, k)
            for k, (source, dest) in enumerate(pairs)
        ]

    def send_planes(field, send_sem, recv_sem):
        top, bottom = pl.ds(last - 8, 8), pl.ds(first, 8)
        before, after = pl.ds(first - 8, 8), pl.ds(last, 8)
        mid = pl.ds(2, 2)
        pairs = (
            (field.at[mid, own_span], field.at[pl.ds(0, 2), own_span]),
            (field.at[mid, own_span], field.at[pl.ds(4, 2), own_span]),
            (field.at[mid, top], field.at[mid, before]),
            (field.at[mid, bottom], field.at[mid, after]),
            (field.at[3, top], field.at[1, before]),
            (field.at[3, bottom], field.at[1, after]),
            (field.at[2, top], field.at[4, before]),
            (field.at[2, bottom], field.at[4, after]),
        )
        return [
            send(source, dest, send_sem, recv_sem, k)
            for k, (source, dest) in enumerate(pairs)
        ]

    comp = lax.broadcasted_iota(jnp.int32, (8, 128), 0)
    lane = lax.broadcasted_iota(jnp.int32, (8, 128), 1)

    for row in range(2):
        for part, ref in enumerate((pos_ref, vel_ref)):
            for axis in range(3):
                value = ref[axis, row]
                for col in range(8):
                    tiles_a[row + 1, col + 1, pl.ds(3 * part + axis, 1), :] = value[
                        col : col + 1
                    ]
        for col in range(8):
            tiles_a[row + 1, col + 1, pl.ds(6, 2), :] = jnp.zeros((2, 128), F32)

    blocks_vec = jnp.full((8, 128), -1, jnp.int32)
    for tile in range(16):
        blocks_vec = jnp.where(
            (lane < 48) & (lax.rem(lane, 16) == tile),
            blocks_ref[tile // 8, tile % 8],
            blocks_vec,
        )
    block_row[8] = blocks_vec.astype(F32)

    span = (2.0 * spring / cutoff_sq) ** 0.5

    def features(tiles, row, col, edge):
        tile = tiles[row, col]
        if edge is not None:
            tile = jnp.where(edge, tile, 0.0)
        shift_x = (col - 4.5) if isinstance(col, int) else (col.astype(F32) - 4.5)
        shift_z = (row - 1.5) if isinstance(row, int) else (row.astype(F32) - 1.5)
        shift = jnp.where(comp == 0, shift_x, jnp.where(comp == 2, shift_z, 0.0))
        at = tile + shift
        speed = pltpu.roll(tile, 5, 0)
        moving = at - damping * speed
        unit = jnp.where(comp < 3, span * at, 0.0)
        half = -0.5 * jnp.sum(unit * unit, axis=0, keepdims=True)
        gram = jnp.where(comp == 3, half, jnp.where(comp == 4, 1.0, unit))
        g_high, g_mid, g_low = split3(gram)
        lanes = pl.ds(col * 128, 128)
        if not isinstance(col, int):
            lanes = pl.ds(pl.multiple_of(col * 128, 128), 128)
        grams[row, :, lanes] = jnp.concatenate(
            [g_high, g_mid, g_high, g_mid, g_low, g_high], axis=0
        ).astype(BF16)
        pull = jnp.where(comp < 3, moving, jnp.where(comp == 3, 1.0, 0.0))
        pull = jnp.where(comp < 4, pull, pltpu.roll(pull, 4, 0))
        products = [
            pull * jnp.where(comp < 4, unit[0:1], unit[1:2]),
            pull * jnp.where(comp < 4, unit[2:3], half),
            jnp.where(comp < 4, pull, 0.0),
        ]
        parts = [split3(product) for product in products]
        pulls[row, :, lanes] = jnp.concatenate(
            [part[level] for level in range(3) for part in parts]
            + [jnp.zeros((8, 128), F32)],
            axis=0,
        ).astype(BF16)
        return unit, half

    def own_features(tiles, row, col):
        unit, half = features(tiles, row + 1, col + 1, None)
        gram = jnp.where(comp == 4, half + spring, jnp.where(comp == 3, 1.0, unit))
        f_high, f_mid, f_low = split3(gram)
        block = jnp.concatenate([f_high, f_high, f_mid, f_mid, f_high, f_low], axis=0)
        owns[col, pl.ds(row * 128, 128), :] = jnp.transpose(
            jnp.concatenate([block, jnp.zeros((80, 128), F32)], axis=0)
        )[:, :48].astype(BF16)

    def gather(jobs):
        steps = []
        for rows, col, pieces, fresh in jobs:
            blocks = [
                (other, step)
                for other, start, count in pieces
                for step in range(start, start + count)
            ]
            for at in range(0, len(blocks), 6):
                last = at + 6 >= len(blocks)
                steps.append((rows, col, blocks[at : at + 6], at == 0, last, fresh))

        def stack(table, col, group):
            parts = []
            for other, step in group:
                begin = (col + step) * 128
                if not isinstance(col, int):
                    begin = pl.multiple_of(begin, 128)
                parts.append(table[other, :, pl.ds(begin, 128)])
            return jnp.concatenate(parts, 1)

        def score(rows, col, group, *_):
            mine = owns[col, rows[0] * 128 : (rows[-1] + 1) * 128, :]
            return jnp.dot(mine, stack(grams, col, group), preferred_element_type=F32)

        ready = [score(*step) for step in steps[:1]]
        result = None
        for n, (rows, col, group, begins, ends, fresh) in enumerate(steps):
            if n + 1 < len(steps):
                ready.append(score(*steps[n + 1]))
            scores = ready.pop(0)
            kept = []
            for k, row in enumerate(rows):
                parts = []
                for m, (other, step) in enumerate(group):
                    flag = contacts_ref[row, col, (other - row) * 3 + step].astype(F32)
                    here = scores[k * 128 : (k + 1) * 128, m * 128 : (m + 1) * 128]
                    parts.append(jnp.where(here > 0.0, flag, 0.0).astype(BF16))
                kept.append(jnp.concatenate(parts, 1))
            part = lax.dot_general(
                jnp.concatenate(kept, 0),
                stack(pulls, col, group),
                NT_DIMS,
                preferred_element_type=F32,
            )
            result = part if begins else result + part
            if ends:
                span_p = slice(rows[0] * 128, (rows[-1] + 1) * 128)
                if not fresh:
                    result = result + total[col, span_p, 0:80]
                total[col, span_p, 0:80] = result

    def own_tiles(tiles):
        def make(index, carry):
            own_features(tiles, 0, index)
            own_features(tiles, 1, index)
            return carry

        lax.fori_loop(0, 8, make, 0, unroll=2)

    def near():
        both = (0, 1)
        gather(
            [
                (both, 0, ((1, 1, 2), (2, 1, 2)), True),
                (both, 7, ((1, 0, 2), (2, 0, 2)), True),
            ]
        )

        def inner(index, carry):
            cols = [index * 2 + 1 + k for k in range(2)]
            gather([(both, col, ((1, 0, 3), (2, 0, 3)), True) for col in cols])
            return carry

        lax.fori_loop(0, 6 // 2, inner, 0)

    has_up, has_down = h < high - 1, h > 0
    has_right, has_left = c < wide - 1, c > 0

    def far(tiles):
        def beside(row, carry):
            features(tiles, row, 0, has_left)
            features(tiles, row, 9, has_right)
            return carry

        lax.fori_loop(1, 3, beside, 0)
        features(tiles, 0, 0, has_left & has_down)
        features(tiles, 0, 9, has_right & has_down)
        features(tiles, 3, 0, has_left & has_up)
        features(tiles, 3, 9, has_right & has_up)

        def above(col, carry):
            features(tiles, 0, col, has_down)
            features(tiles, 3, col, has_up)
            return carry

        lax.fori_loop(1, 9, above, 0, unroll=2)

        def inner(index, carry):
            jobs = []
            for k in range(2):
                jobs.append(((0,), index * 2 + 1 + k, ((0, 0, 3),), False))
                jobs.append(((1,), index * 2 + 1 + k, ((3, 0, 3),), False))
            gather(jobs)
            return carry

        lax.fori_loop(0, 6 // 2, inner, 0)
        jobs = []
        for row in range(2):
            jobs.append(((row,), 0, ((3 * row, 0, 3), (1, 0, 1), (2, 0, 1)), False))
            jobs.append(((row,), 7, ((3 * row, 0, 3), (1, 2, 1), (2, 2, 1)), False))
        gather(jobs)

    def advanced(tiles, row, col):
        tile = tiles[row + 1, col + 1]
        sums = jnp.transpose(total[col, pl.ds(row * 128, 128), :])
        sums = sums[0:24] + sums[24:48] + sums[48:72]
        shift = jnp.where(
            comp == 0,
            col.astype(F32) - 3.5,
            jnp.where(comp == 2, row - 0.5, 0.0),
        )
        at = tile + shift
        moving = at - damping * pltpu.roll(tile, 5, 0)
        unit = jnp.where(comp < 3, span * at, 0.0)
        half = -0.5 * jnp.sum(unit * unit, axis=0, keepdims=True)
        pulled = (
            sums[0:8] * jnp.where(comp < 4, unit[0:1], unit[1:2])
            + sums[8:16] * jnp.where(comp < 4, unit[2:3], 1.0)
            + sums[16:24] * (half + spring)
        )
        pulled = pulled + pltpu.roll(pulled, 4, 0)
        force = pltpu.roll(moving * pulled[3:4] - pulled, 3, 0)
        speeds = tile + step_dt * force - jnp.where(comp == 5, step_dt * gravity, 0.0)
        places = tile + step_dt * pltpu.roll(speeds, 5, 0)
        return jnp.where(comp < 3, places, jnp.where(comp < 6, speeds, 0.0))

    pl.semaphore_wait(barrier, len(greeted))

    halo_a = send_tiles(tiles_a, send_a, recv_a)
    load_gas.wait()
    load_diag.wait()
    halo_gas = send_planes(gas, send_gas, recv_gas)
    halo_blk = [
        send(block_row.at[8], block_row.at[k], send_blk, recv_blk, k) for k in range(8)
    ]
    spread()
    own_tiles(tiles_a)
    near()
    for copy in halo_a:
        copy.wait_recv()
    spread()
    far(tiles_a)
    spread()

    def first_step(col, carry):
        tiles_b[1, col + 1] = advanced(tiles_a, 0, col)
        tiles_b[2, col + 1] = advanced(tiles_a, 1, col)
        return carry

    lax.fori_loop(0, 8, first_step, 0, unroll=4)
    halo_b = send_tiles(tiles_b, send_b, recv_b)
    halo_diag = send_planes(scale, send_diag, recv_diag)
    own_tiles(tiles_b)
    near()
    spread()

    def invert(place_p, place_r, rows, valid):
        for row in range(place_r, place_r + rows, 8):
            m = 1.0 / (6.0 + scale[place_p, row : row + 8, :])
            if valid is not None:
                m = jnp.where(valid, m, 0.0)
            recip[place_p, row : row + 8, :] = m

    invert(2, first, own_rows, None)
    invert(3, first, own_rows, None)
    for copy in halo_b:
        copy.wait_recv()
    far(tiles_b)
    spread()

    count_row = lax.broadcasted_iota(jnp.int32, (128, 128), 0)

    def second_step(col, carry):
        for row in range(2):
            tile = advanced(tiles_b, row, col)
            settled[row * 8 + col] = tile
            lift = deposit_gain * tile[5:6]
            l_high, l_mid, l_low = split3(lift)
            rows = jnp.where(
                comp == 0,
                l_high,
                jnp.where(comp == 1, l_mid, jnp.where(comp == 2, l_low, 0.0)),
            )
            slot = slots_ref[row, pl.ds(col, 1), :]
            table = jnp.where(count_row == slot, 1.0, 0.0).astype(BF16)
            placed = lax.dot_general(
                jnp.concatenate([rows, jnp.zeros((8, 128), F32)], axis=0).astype(BF16),
                table,
                NT_DIMS,
                preferred_element_type=F32,
            )
            per_tile[8, pl.ds(row * 8 + col, 1), :] = jnp.sum(
                placed[0:8], axis=0, keepdims=True
            )
        return carry

    lax.fori_loop(0, 8, second_step, 0, unroll=4)
    halo_dep = [
        send(per_tile.at[8], per_tile.at[k], send_dep, recv_dep, k) for k in range(8)
    ]

    rank = jnp.int32(0)
    picks = [[None] * 8 for _ in range(8)]
    stays = []
    for col in range(8):
        flag = exit_ref[1, col]
        for k in range(8):
            picks[k][col] = jnp.where(rank == k, flag, 0).astype(F32)
        stays.append((1 - flag).astype(F32))
        rank = rank + flag
    for k in range(8):
        value = picks[k][0] * settled[8]
        for col in range(1, 8):
            value = value + picks[k][col] * settled[8 + col]
        leaving[k] = value
    move = pltpu.make_async_remote_copy(
        src_ref=leaving,
        dst_ref=arrived,
        send_sem=send_mig.at[0],
        recv_sem=recv_mig.at[0],
        device_id=(up, c),
        device_id_type=MESH,
    )
    move.start()

    for copy in halo_gas:
        copy.wait_recv()
    for copy in halo_diag:
        copy.wait_recv()
    for copy in halo_gas:
        copy.wait_send()
    for copy in halo_blk:
        copy.wait_recv()

    def enter(source, place_p, place_r, from_p, from_r, rows):
        parts = jnp.concatenate(
            list(split3(per_tile[source])) + [jnp.zeros((80, 128), F32)], axis=0
        ).astype(BF16)
        owners = block_row[source][0:1]
        base = lax.broadcasted_iota(jnp.int32, (rows, 128), 0)
        for quarter in range(4):
            number = ((base + (from_p * own_rows + from_r)) * 4 + quarter).astype(F32)
            table = jnp.where(number == owners, 1.0, 0.0).astype(BF16)
            lanes = slice(quarter * 128, (quarter + 1) * 128)
            r0 = gas[place_p, place_r : place_r + rows, lanes] - jnp.dot(
                table, parts, preferred_element_type=F32
            )
            m = recip[place_p, place_r : place_r + rows, lanes]
            gas[place_p, place_r : place_r + rows, lanes] = r0
            zed[place_p, place_r : place_r + rows, lanes] = m * r0

    far_row = own_rows - 8
    enter(8, 2, first, 0, 0, own_rows)
    enter(8, 3, first, 1, 0, own_rows)
    invert(0, first, own_rows, has_down)
    invert(1, first, own_rows, has_down)
    invert(4, first, own_rows, has_up)
    invert(5, first, own_rows, has_up)
    for p in range(2):
        invert(2 + p, first - 8, 8, has_left)
        invert(2 + p, last, 8, has_right)
    invert(1, first - 8, 8, has_left & has_down)
    invert(1, last, 8, has_right & has_down)
    invert(4, first - 8, 8, has_left & has_up)
    invert(4, last, 8, has_right & has_up)
    for copy in halo_dep:
        copy.wait_recv()
    enter(0, 0, first, 0, 0, own_rows)
    enter(0, 1, first, 1, 0, own_rows)
    enter(1, 4, first, 0, 0, own_rows)
    enter(1, 5, first, 1, 0, own_rows)
    for p in range(2):
        enter(2, 2 + p, first - 8, p, far_row, 8)
        enter(3, 2 + p, last, p, 0, 8)
    enter(4, 1, first - 8, 1, far_row, 8)
    enter(5, 1, last, 1, 0, 8)
    enter(6, 4, first - 8, 0, far_row, 8)
    enter(7, 4, last, 0, 0, 8)

    lane_w = lax.broadcasted_iota(jnp.int32, (8, 512), 1)

    def beside_sum(field, p, row):
        here = field[p, row : row + 8, :]
        ahead = jnp.where(lane_w == 0, 0.0, pltpu.roll(here, 1, 1))
        behind = jnp.where(lane_w == 511, 0.0, pltpu.roll(here, 511, 1))
        result = field[p + 1, row : row + 8, :] + field[p - 1, row : row + 8, :]
        result = result + field[p, row + 1 : row + 9, :]
        result = result + field[p, row - 1 : row + 7, :]
        return result + ahead + behind

    zero = jnp.zeros((8, 512), F32)
    dots = [zero, zero, zero, zero]
    for p in (2, 3, 1, 4):
        inside = p in (2, 3)
        start, stop = (first - 8, last + 8) if inside else (first, last)
        for row in range(start, stop, 8):
            r0 = gas[p, row : row + 8, :]
            u = r0 - beside_sum(zed, p, row)
            w = recip[p, row : row + 8, :] * u
            weighed[p, row : row + 8, :] = w
            if inside and first <= row < last:
                image[p, row : row + 8, :] = u
                z0 = zed[p, row : row + 8, :]
                dots[0] = dots[0] + r0 * z0
                dots[1] = dots[1] + z0 * u
                dots[2] = dots[2] + u * w
    for p in (2, 3):
        for row in range(first, last, 8):
            t = image[p, row : row + 8, :] - beside_sum(weighed, p, row)
            twice[p - 2, row - first : row - first + 8, :] = t
            dots[3] = dots[3] + weighed[p, row : row + 8, :] * t

    lane_one = lax.broadcasted_iota(jnp.int32, (1, 128), 1)
    mine = jnp.zeros((1, 128), F32)
    for k, dot in enumerate(dots):
        fold = jnp.sum(dot, axis=0, keepdims=True)
        fold = fold[:, 0:128] + fold[:, 128:256] + fold[:, 256:384] + fold[:, 384:512]
        fold = fold + pltpu.roll(fold, 64, 1)
        fold = fold + pltpu.roll(fold, 32, 1)
        mine = jnp.where(lane_one // 32 == k, fold, mine)
    row_a[0] = mine

    def share(peers, source, slots, send_sem, recv_sem):
        copies = []
        for k, target in enumerate(peers):
            copies.append(
                pltpu.make_async_remote_copy(
                    src_ref=source.at[0],
                    dst_ref=slots.at[k],
                    send_sem=send_sem.at[k],
                    recv_sem=recv_sem.at[k],
                    device_id=target,
                    device_id_type=MESH,
                )
            )
            copies[-1].start()
        return copies

    sums_a = share(peers_a, row_a, rows_a, send_ra, recv_ra)
    stores = [
        pltpu.make_async_copy(
            gas.at[pl.ds(2, 2), own_span], right_out, store_sem.at[0]
        ),
        pltpu.make_async_copy(
            image.at[pl.ds(2, 2), own_span], image_out, store_sem.at[1]
        ),
        pltpu.make_async_copy(twice, twice_out, store_sem.at[2]),
    ]
    for copy in stores:
        copy.start()

    move.wait()
    targets = [inlet_ref[0, k] for k in range(8)]
    for col in range(8):
        value = jnp.where(targets[0] == col, 1.0, 0.0) * arrived[0]
        for k in range(1, 8):
            value = value + jnp.where(targets[k] == col, 1.0, 0.0) * arrived[k]
        settled[col] = value
        settled[8 + col] = settled[8 + col] * stays[col]
    for row in range(2):
        for part, ref in enumerate((pos_buf, vel_buf)):
            for axis in range(3):
                for col in range(8):
                    ref[axis, row, pl.ds(col, 1), :] = settled[
                        row * 8 + col, pl.ds(3 * part + axis, 1), :
                    ]

    stores += [
        pltpu.make_async_copy(pos_buf, pos_out, store_sem.at[3]),
        pltpu.make_async_copy(vel_buf, vel_out, store_sem.at[4]),
    ]
    for copy in stores[3:]:
        copy.start()
    for copy in halo_a + halo_b + halo_diag + halo_blk + halo_dep:
        copy.wait_send()

    for copy in sums_a:
        copy.wait_recv()
    mine = mine + jnp.sum(rows_a[...], axis=0)
    row_b[0] = mine
    sums_b = share(peers_b, row_b, rows_b, send_rb, recv_rb)
    for copy in sums_a:
        copy.wait_send()
    for copy in stores:
        copy.wait()
    for copy in sums_b:
        copy.wait_recv()
    sums_out[...] = mine + jnp.sum(rows_b[...], axis=0)
    for copy in sums_b:
        copy.wait_send()


def finish(sums, right, image, twice, diag, pos, vel, pos_out, vel_out, press, resid):
    lane = lax.broadcasted_iota(jnp.int32, (1, 128), 1)
    rz, energy, cross, third = (
        jnp.sum(jnp.where(lane // 32 == k, sums[...], 0.0), axis=1, keepdims=True)
        for k in range(4)
    )
    alpha = rz / energy
    renewed = alpha * alpha * cross - rz
    grow = 1.0 + renewed / rz
    second = renewed / (
        grow * grow * energy - 2.0 * grow * alpha * cross + alpha * alpha * third
    )
    near_factor = jnp.broadcast_to(alpha + second * grow, (8, 128))[:, 0:1]
    far_factor = jnp.broadcast_to(second * alpha, (8, 128))[:, 0:1]
    for row in range(0, right.shape[1], 8):
        rows = slice(row, row + 8)
        r0, u = right[0, rows, :], image[0, rows, :]
        m = 1.0 / (6.0 + diag[0, rows, :])
        press[0, rows, :] = m * (near_factor * r0 - far_factor * u)
        resid[0, rows, :] = r0 - near_factor * u + far_factor * twice[0, rows, :]

    @pl.when(pl.program_id(0) + pl.program_id(1) == 0)
    def _():
        pos_out[...] = pos[...]
        vel_out[...] = vel[...]


def on_device(
    depth_z,
    positions,
    velocities,
    contacts,
    exit_flags,
    inlet_slots,
    cell_blocks,
    cell_slots,
    gas_source,
    diagonal,
):
    high = lax.axis_size("height")
    count_a = 2 * depth_z - 1
    count_b = (high // (2 * depth_z)) * lax.axis_size("cols") - 1
    vmem = pl.BlockSpec(memory_space=pltpu.VMEM)
    smem = pl.BlockSpec(memory_space=pltpu.SMEM)
    hbm = pl.BlockSpec(memory_space=pl.ANY)
    dma = pltpu.SemaphoreType.DMA
    own_rows = gas_source.shape[1]
    grid = (6, own_rows + 2 * PAD, gas_source.shape[2])
    field = jax.ShapeDtypeStruct(gas_source.shape, F32)
    state = jax.ShapeDtypeStruct(positions.shape, F32)
    row = jax.ShapeDtypeStruct((1, 128), F32)
    pos, vel, right, image, twice, sums = pl.pallas_call(
        functools.partial(kernel, depth_z),
        out_shape=(state, state, field, field, field, row),
        in_specs=[vmem, vmem, vmem, smem, smem, smem, smem, hbm, hbm],
        out_specs=(hbm, hbm, hbm, hbm, hbm, vmem),
        scratch_shapes=[
            pltpu.VMEM(positions.shape, F32),
            pltpu.VMEM(positions.shape, F32),
            pltpu.VMEM((4, 10, 8, 128), F32),
            pltpu.VMEM((4, 10, 8, 128), F32),
            pltpu.VMEM((4, 48, 1280), BF16),
            pltpu.VMEM((4, 80, 1280), BF16),
            pltpu.VMEM((8, 256, 48), BF16),
            pltpu.VMEM((8, 256, 128), F32),
            pltpu.VMEM((16, 8, 128), F32),
            pltpu.VMEM(grid, F32),
            pltpu.VMEM(grid, F32),
            pltpu.VMEM(grid, F32),
            pltpu.VMEM(grid, F32),
            pltpu.VMEM(grid, F32),
            pltpu.VMEM(grid, F32),
            pltpu.VMEM(gas_source.shape, F32),
            pltpu.VMEM((9, 16, 128), F32),
            pltpu.VMEM((9, 8, 128), F32),
            pltpu.VMEM((8, 8, 128), F32),
            pltpu.VMEM((8, 8, 128), F32),
            pltpu.VMEM((1, 1, 128), F32),
            pltpu.VMEM((count_a, 1, 128), F32),
            pltpu.VMEM((1, 1, 128), F32),
            pltpu.VMEM((count_b, 1, 128), F32),
            dma((2,)),
            dma((5,)),
            pltpu.SemaphoreType.REGULAR((8,)),
            pltpu.SemaphoreType.REGULAR((8,)),
            dma((8,)),
            dma((8,)),
            dma((8,)),
            dma((8,)),
            dma((8,)),
            dma((8,)),
            dma((8,)),
            dma((8,)),
            dma((8,)),
            dma((8,)),
            dma((8,)),
            dma((8,)),
            dma((1,)),
            dma((1,)),
            dma((count_a,)),
            dma((count_a,)),
            dma((count_b,)),
            dma((count_b,)),
        ],
        compiler_params=pltpu.CompilerParams(
            collective_id=0, has_side_effects=True
        ),
    )(
        positions,
        velocities,
        cell_slots,
        jnp.transpose(contacts, (1, 2, 0)),
        exit_flags,
        inlet_slots,
        cell_blocks,
        gas_source,
        diagonal,
    )
    whole = pl.BlockSpec(positions.shape, lambda p, q: (0, 0, 0, 0))
    part = pl.BlockSpec(
        (1, own_rows // 2, gas_source.shape[2]), lambda p, q: (p, q, 0)
    )
    return pl.pallas_call(
        finish,
        grid=(2, 2),
        out_shape=(state, state, field, field),
        in_specs=[pl.BlockSpec((1, 128), lambda p, q: (0, 0))]
        + [part] * 4
        + [whole] * 2,
        out_specs=(whole, whole, part, part),
    )(sums, right, image, twice, diagonal, pos, vel)


def solution(mesh, depth_z=16):
    in_specs = (
        P(None, "height", "cols", None),
        P(None, "height", "cols", None),
        P(None, "height", "cols"),
        P("height", "cols"),
        P("height", "cols"),
        P("height", "cols"),
        P("height", "cols", None),
        P("height", "cols", None),
        P("height", "cols", None),
    )
    out_specs = (
        P(None, "height", "cols", None),
        P(None, "height", "cols", None),
        P("height", "cols", None),
        P("height", "cols", None),
    )
    return jax.shard_map(
        functools.partial(on_device, depth_z),
        mesh=mesh,
        in_specs=in_specs,
        out_specs=out_specs,
        check_vma=False,
    )
```

```python
import functools

import jax
import jax.numpy as jnp
from jax import lax
from jax.experimental import pallas as pl
from jax.experimental.pallas import tpu as pltpu
from jax.sharding import PartitionSpec as P

MESH = pl.DeviceIdType.MESH
F32 = jnp.float32
BF16 = jnp.bfloat16

spring = 0.05
cutoff_sq = 1.44
damping = 0.5
step_dt = 0.05
gravity = 1.0
deposit_gain = 2.0

PAD = 16
NT_DIMS = (((1,), (1,)), ((), ()))
TN_DIMS = (((0,), (0,)), ((), ()))


def split3(value):
    high = value.astype(BF16).astype(F32)
    rest = value - high
    mid = rest.astype(BF16).astype(F32)
    return high, mid, (rest - mid).astype(BF16).astype(F32)


def kernel(
    depth_z,
    pos_ref,
    vel_ref,
    slots_ref,
    contacts_ref,
    exit_ref,
    inlet_ref,
    blocks_ref,
    gas_ref,
    diag_ref,
    pos_out,
    vel_out,
    right_out,
    image_out,
    twice_out,
    sums_out,
    pos_buf,
    vel_buf,
    tiles_a,
    tiles_b,
    grams,
    pulls,
    owns,
    total,
    settled,
    gas,
    scale,
    recip,
    zed,
    image,
    weighed,
    twice,
    per_tile,
    block_row,
    leaving,
    arrived,
    row_a,
    rows_a,
    row_b,
    rows_b,
    load_sem,
    store_sem,
    known_z,
    known_p,
    send_a,
    recv_a,
    send_b,
    recv_b,
    send_gas,
    recv_gas,
    send_diag,
    recv_diag,
    send_blk,
    recv_blk,
    send_dep,
    recv_dep,
    send_mig,
    recv_mig,
    send_ra,
    recv_ra,
    send_rb,
    recv_rb,
):
    high = lax.axis_size("height")
    wide = lax.axis_size("cols")
    h = lax.axis_index("height")
    c = lax.axis_index("cols")
    up = lax.rem(h + 1, high)
    down = lax.rem(h + high - 1, high)
    right = lax.rem(c + 1, wide)
    left = lax.rem(c + wide - 1, wide)
    goes = (
        (up, c),
        (down, c),
        (h, right),
        (h, left),
        (up, right),
        (up, left),
        (down, right),
        (down, left),
    )
    core = lax.rem(h, 2)
    z = lax.rem(h // 2, depth_z)
    x = h // (2 * depth_z)
    depth_x = high // (2 * depth_z)

    def z_peer(step):
        return (x * depth_z + lax.rem(z + step, depth_z)) * 2 + core

    def x_peer(step):
        return (lax.rem(x + step, depth_x) * depth_z + z) * 2 + core

    def y_peer(step):
        return lax.rem(c + step, wide)

    def far_first(steps, count):
        return sorted(steps, key=lambda step: -min(step, count - step))

    line_z = [z_peer(step) if step else h for step in range(depth_z)]
    line_x = [x_peer(step) if step else h for step in range(depth_x)]
    line_y = [y_peer(step) if step else c for step in range(wide)]
    other_core = 1 - 2 * core
    peers_a = [
        (line_z[step] + flip * other_core, c)
        for step in far_first(range(depth_z), depth_z)
        for flip in range(2)
        if step or flip
    ]
    peers_b = [
        (line_x[step_x], line_y[step_y])
        for step_y in far_first(range(wide), wide)
        for step_x in far_first(range(depth_x), depth_x)
        if step_x or step_y
    ]

    def signal(sem, target):
        pl.semaphore_signal(sem, inc=1, device_id=target, device_id_type=MESH)

    chain_z, chain_p = [], []
    reach = 1
    while reach < depth_z // 2:
        chain_z.append(((z_peer(reach), c), (z_peer(depth_z - reach), c)))
        reach *= 2
    chain_z.append(((h + other_core, c),))
    reach = 1
    while reach < wide // 2:
        chain_p.append(((h, y_peer(reach)), (h, y_peer(wide - reach))))
        reach *= 2
    for _ in range(depth_x // 2):
        chain_p.append(((x_peer(1), c), (x_peer(depth_x - 1), c)))
    stage = [0]

    def spread():
        now = stage[0]
        for chain, sem in ((chain_z, known_z), (chain_p, known_p)):
            if 0 < now <= len(chain):
                pl.semaphore_wait(sem.at[now - 1], len(chain[now - 1]))
        for chain, sem in ((chain_z, known_z), (chain_p, known_p)):
            if now < len(chain):
                for target in chain[now]:
                    signal(sem.at[now], target)
        stage[0] = now + 1

    own_rows = gas_ref.shape[1]
    first, last = PAD, PAD + own_rows
    own_span = pl.ds(first, own_rows)
    load_gas = pltpu.make_async_copy(
        gas_ref, gas.at[pl.ds(2, 2), own_span], load_sem.at[0]
    )
    load_diag = pltpu.make_async_copy(
        diag_ref, scale.at[pl.ds(2, 2), own_span], load_sem.at[1]
    )
    load_gas.start()
    load_diag.start()

    barrier = pltpu.get_barrier_semaphore()
    greeted = goes + (
        (z_peer(1), c),
        (z_peer(depth_z - 1), c),
        (x_peer(1), c),
        (x_peer(depth_x - 1), c),
    )
    for target in greeted:
        signal(barrier, target)

    def send(source, dest, send_sem, recv_sem, k):
        copy = pltpu.make_async_remote_copy(
            src_ref=source,
            dst_ref=dest,
            send_sem=send_sem.at[k],
            recv_sem=recv_sem.at[k],
            device_id=goes[k],
            device_id_type=MESH,
        )
        copy.start()
        return copy

    def send_tiles(tiles, send_sem, recv_sem):
        pairs = (
            (tiles.at[2, pl.ds(1, 8)], tiles.at[0, pl.ds(1, 8)]),
            (tiles.at[1, pl.ds(1, 8)], tiles.at[3, pl.ds(1, 8)]),
            (tiles.at[pl.ds(1, 2), 8], tiles.at[pl.ds(1, 2), 0]),
            (tiles.at[pl.ds(1, 2), 1], tiles.at[pl.ds(1, 2), 9]),
            (tiles.at[2, 8], tiles.at[0, 0]),
            (tiles.at[2, 1], tiles.at[0, 9]),
            (tiles.at[1, 8], tiles.at[3, 0]),
            (tiles.at[1, 1], tiles.at[3, 9]),
        )
        return [
            send(source, dest, send_sem, recv_sem, k)
            for k, (source, dest) in reversed(list(enumerate(pairs)))
        ]

    def send_planes(field, send_sem, recv_sem):
        top, bottom = pl.ds(last - 8, 8), pl.ds(first, 8)
        before, after = pl.ds(first - 8, 8), pl.ds(last, 8)
        mid = pl.ds(2, 2)
        pairs = (
            (field.at[mid, own_span], field.at[pl.ds(0, 2), own_span]),
            (field.at[mid, own_span], field.at[pl.ds(4, 2), own_span]),
            (field.at[mid, top], field.at[mid, before]),
            (field.at[mid, bottom], field.at[mid, after]),
            (field.at[3, top], field.at[1, before]),
            (field.at[3, bottom], field.at[1, after]),
            (field.at[2, top], field.at[4, before]),
            (field.at[2, bottom], field.at[4, after]),
        )
        return [
            send(source, dest, send_sem, recv_sem, k)
            for k, (source, dest) in reversed(list(enumerate(pairs)))
        ]

    comp = lax.broadcasted_iota(jnp.int32, (8, 128), 0)
    lane = lax.broadcasted_iota(jnp.int32, (8, 128), 1)

    for row in range(2):
        for part, ref in enumerate((pos_ref, vel_ref)):
            for axis in range(3):
                value = ref[axis, row]
                for col in range(8):
                    tiles_a[row + 1, col + 1, pl.ds(3 * part + axis, 1), :] = value[
                        col : col + 1
                    ]
        for col in range(8):
            tiles_a[row + 1, col + 1, pl.ds(6, 2), :] = jnp.zeros((2, 128), F32)

    blocks_vec = jnp.full((8, 128), -1, jnp.int32)
    for tile in range(16):
        blocks_vec = jnp.where(
            (lane < 48) & (lax.rem(lane, 16) == tile),
            blocks_ref[tile // 8, tile % 8],
            blocks_vec,
        )
    block_row[8] = blocks_vec.astype(F32)

    span = (2.0 * spring / cutoff_sq) ** 0.5

    def features(tiles, row, col, edge):
        tile = tiles[row, col]
        if edge is not None:
            tile = jnp.where(edge, tile, 0.0)
        shift_x = (col - 4.5) if isinstance(col, int) else (col.astype(F32) - 4.5)
        shift_z = (row - 1.5) if isinstance(row, int) else (row.astype(F32) - 1.5)
        shift = jnp.where(comp == 0, shift_x, jnp.where(comp == 2, shift_z, 0.0))
        at = tile + shift
        speed = pltpu.roll(tile, 5, 0)
        moving = at - damping * speed
        unit = jnp.where(comp < 3, span * at, 0.0)
        half = -0.5 * jnp.sum(unit * unit, axis=0, keepdims=True)
        gram = jnp.where(comp == 3, half, jnp.where(comp == 4, 1.0, unit))
        g_high, g_mid, g_low = split3(gram)
        lanes = pl.ds(col * 128, 128)
        if not isinstance(col, int):
            lanes = pl.ds(pl.multiple_of(col * 128, 128), 128)
        grams[row, :, lanes] = jnp.concatenate(
            [g_high, g_mid, g_high, g_mid, g_low, g_high], axis=0
        ).astype(BF16)
        pull = jnp.where(comp < 3, moving, jnp.where(comp == 3, 1.0, 0.0))
        pull = jnp.where(comp < 4, pull, pltpu.roll(pull, 4, 0))
        products = [
            pull * jnp.where(comp < 4, unit[0:1], unit[1:2]),
            pull * jnp.where(comp < 4, unit[2:3], half),
            jnp.where(comp < 4, pull, 0.0),
        ]
        parts = [split3(product) for product in products]
        pulls[row, :, lanes] = jnp.concatenate(
            [part[level] for level in range(3) for part in parts]
            + [jnp.zeros((8, 128), F32)],
            axis=0,
        ).astype(BF16)
        return unit, half

    def own_features(tiles, row, col):
        unit, half = features(tiles, row + 1, col + 1, None)
        gram = jnp.where(comp == 4, half + spring, jnp.where(comp == 3, 1.0, unit))
        f_high, f_mid, f_low = split3(gram)
        block = jnp.concatenate([f_high, f_high, f_mid, f_mid, f_high, f_low], axis=0)
        owns[col, pl.ds(row * 128, 128), :] = jnp.transpose(
            jnp.concatenate([block, jnp.zeros((80, 128), F32)], axis=0)
        )[:, :48].astype(BF16)

    def gather(jobs):
        steps = []
        for rows, col, pieces, fresh in jobs:
            blocks = [
                (other, step)
                for other, start, count in pieces
                for step in range(start, start + count)
            ]
            for at in range(0, len(blocks), 6):
                last = at + 6 >= len(blocks)
                steps.append((rows, col, blocks[at : at + 6], at == 0, last, fresh))

        def stack(table, col, group):
            parts = []
            for other, step in group:
                begin = (col + step) * 128
                if not isinstance(col, int):
                    begin = pl.multiple_of(begin, 128)
                parts.append(table[other, :, pl.ds(begin, 128)])
            return jnp.concatenate(parts, 1)

        def score(rows, col, group, *_):
            mine = owns[col, rows[0] * 128 : (rows[-1] + 1) * 128, :]
            return jnp.dot(mine, stack(grams, col, group), preferred_element_type=F32)

        ready = [score(*step) for step in steps[:1]]
        result = None
        for n, (rows, col, group, begins, ends, fresh) in enumerate(steps):
            if n + 1 < len(steps):
                ready.append(score(*steps[n + 1]))
            scores = ready.pop(0)
            kept = []
            for k, row in enumerate(rows):
                parts = []
                for m, (other, step) in enumerate(group):
                    flag = contacts_ref[row, col, (other - row) * 3 + step].astype(F32)
                    here = scores[k * 128 : (k + 1) * 128, m * 128 : (m + 1) * 128]
                    parts.append(jnp.where(here > 0.0, flag, 0.0).astype(BF16))
                kept.append(jnp.concatenate(parts, 1))
            part = lax.dot_general(
                jnp.concatenate(kept, 0),
                stack(pulls, col, group),
                NT_DIMS,
                preferred_element_type=F32,
            )
            result = part if begins else result + part
            if ends:
                span_p = slice(rows[0] * 128, (rows[-1] + 1) * 128)
                if not fresh:
                    result = result + total[col, span_p, 0:80]
                total[col, span_p, 0:80] = result

    def own_tiles(tiles):
        def make(index, carry):
            own_features(tiles, 0, index)
            own_features(tiles, 1, index)
            return carry

        lax.fori_loop(0, 8, make, 0, unroll=2)

    def near():
        both = (0, 1)
        gather(
            [
                (both, 0, ((1, 1, 2), (2, 1, 2)), True),
                (both, 7, ((1, 0, 2), (2, 0, 2)), True),
            ]
        )

        def inner(index, carry):
            cols = [index * 2 + 1 + k for k in range(2)]
            gather([(both, col, ((1, 0, 3), (2, 0, 3)), True) for col in cols])
            return carry

        lax.fori_loop(0, 6 // 2, inner, 0)

    has_up, has_down = h < high - 1, h > 0
    has_right, has_left = c < wide - 1, c > 0

    def far(tiles):
        def beside(row, carry):
            features(tiles, row, 0, has_left)
            features(tiles, row, 9, has_right)
            return carry

        lax.fori_loop(1, 3, beside, 0)
        features(tiles, 0, 0, has_left & has_down)
        features(tiles, 0, 9, has_right & has_down)
        features(tiles, 3, 0, has_left & has_up)
        features(tiles, 3, 9, has_right & has_up)

        def above(col, carry):
            features(tiles, 0, col, has_down)
            features(tiles, 3, col, has_up)
            return carry

        lax.fori_loop(1, 9, above, 0, unroll=2)

        def inner(index, carry):
            jobs = []
            for k in range(2):
                jobs.append(((0,), index * 2 + 1 + k, ((0, 0, 3),), False))
                jobs.append(((1,), index * 2 + 1 + k, ((3, 0, 3),), False))
            gather(jobs)
            return carry

        lax.fori_loop(0, 6 // 2, inner, 0)
        jobs = []
        for row in range(2):
            jobs.append(((row,), 0, ((3 * row, 0, 3), (1, 0, 1), (2, 0, 1)), False))
            jobs.append(((row,), 7, ((3 * row, 0, 3), (1, 2, 1), (2, 2, 1)), False))
        gather(jobs)

    def advanced(tiles, row, col):
        tile = tiles[row + 1, col + 1]
        sums = jnp.transpose(total[col, pl.ds(row * 128, 128), :])
        sums = sums[0:24] + sums[24:48] + sums[48:72]
        shift = jnp.where(
            comp == 0,
            col.astype(F32) - 3.5,
            jnp.where(comp == 2, row - 0.5, 0.0),
        )
        at = tile + shift
        moving = at - damping * pltpu.roll(tile, 5, 0)
        unit = jnp.where(comp < 3, span * at, 0.0)
        half = -0.5 * jnp.sum(unit * unit, axis=0, keepdims=True)
        pulled = (
            sums[0:8] * jnp.where(comp < 4, unit[0:1], unit[1:2])
            + sums[8:16] * jnp.where(comp < 4, unit[2:3], 1.0)
            + sums[16:24] * (half + spring)
        )
        pulled = pulled + pltpu.roll(pulled, 4, 0)
        force = pltpu.roll(moving * pulled[3:4] - pulled, 3, 0)
        speeds = tile + step_dt * force - jnp.where(comp == 5, step_dt * gravity, 0.0)
        places = tile + step_dt * pltpu.roll(speeds, 5, 0)
        return jnp.where(comp < 3, places, jnp.where(comp < 6, speeds, 0.0))

    pl.semaphore_wait(barrier, len(greeted))
    spread()

    halo_a = send_tiles(tiles_a, send_a, recv_a)
    load_gas.wait()
    load_diag.wait()
    halo_gas = send_planes(gas, send_gas, recv_gas)
    halo_blk = [
        send(block_row.at[8], block_row.at[k], send_blk, recv_blk, k) for k in range(8)
    ]
    own_tiles(tiles_a)
    near()
    for copy in halo_a:
        copy.wait_recv()
    spread()
    far(tiles_a)
    spread()

    def first_step(col, carry):
        tiles_b[1, col + 1] = advanced(tiles_a, 0, col)
        tiles_b[2, col + 1] = advanced(tiles_a, 1, col)
        return carry

    lax.fori_loop(0, 8, first_step, 0, unroll=4)
    halo_b = send_tiles(tiles_b, send_b, recv_b)
    halo_diag = send_planes(scale, send_diag, recv_diag)
    own_tiles(tiles_b)
    near()
    spread()

    def invert(place_p, place_r, rows, valid):
        for row in range(place_r, place_r + rows, 8):
            m = 1.0 / (6.0 + scale[place_p, row : row + 8, :])
            if valid is not None:
                m = jnp.where(valid, m, 0.0)
            recip[place_p, row : row + 8, :] = m

    invert(2, first, own_rows, None)
    invert(3, first, own_rows, None)
    for copy in halo_b:
        copy.wait_recv()
    far(tiles_b)
    spread()

    count_row = lax.broadcasted_iota(jnp.int32, (128, 128), 0)

    def second_step(col, carry):
        for row in range(2):
            tile = advanced(tiles_b, row, col)
            settled[row * 8 + col] = tile
            lift = deposit_gain * tile[5:6]
            l_high, l_mid, l_low = split3(lift)
            rows = jnp.where(
                comp == 0,
                l_high,
                jnp.where(comp == 1, l_mid, jnp.where(comp == 2, l_low, 0.0)),
            )
            slot = slots_ref[row, pl.ds(col, 1), :]
            table = jnp.where(count_row == slot, 1.0, 0.0).astype(BF16)
            placed = lax.dot_general(
                jnp.concatenate([rows, jnp.zeros((8, 128), F32)], axis=0).astype(BF16),
                table,
                NT_DIMS,
                preferred_element_type=F32,
            )
            per_tile[8, pl.ds(row * 8 + col, 1), :] = jnp.sum(
                placed[0:8], axis=0, keepdims=True
            )
        return carry

    lax.fori_loop(0, 8, second_step, 0, unroll=4)
    halo_dep = [
        send(per_tile.at[8], per_tile.at[k], send_dep, recv_dep, k)
        for k in reversed(range(8))
    ]

    rank = jnp.int32(0)
    picks = [[None] * 8 for _ in range(8)]
    stays = []
    for col in range(8):
        flag = exit_ref[1, col]
        for k in range(8):
            picks[k][col] = jnp.where(rank == k, flag, 0).astype(F32)
        stays.append((1 - flag).astype(F32))
        rank = rank + flag
    for k in range(8):
        value = picks[k][0] * settled[8]
        for col in range(1, 8):
            value = value + picks[k][col] * settled[8 + col]
        leaving[k] = value
    move = pltpu.make_async_remote_copy(
        src_ref=leaving,
        dst_ref=arrived,
        send_sem=send_mig.at[0],
        recv_sem=recv_mig.at[0],
        device_id=(up, c),
        device_id_type=MESH,
    )
    move.start()

    for copy in halo_gas:
        copy.wait_recv()
    for copy in halo_diag:
        copy.wait_recv()
    for copy in halo_gas:
        copy.wait_send()
    for copy in halo_blk:
        copy.wait_recv()

    def enter(source, place_p, place_r, from_p, from_r, rows):
        parts = jnp.concatenate(
            list(split3(per_tile[source])) + [jnp.zeros((80, 128), F32)], axis=0
        ).astype(BF16)
        owners = block_row[source][0:1]
        base = lax.broadcasted_iota(jnp.int32, (rows, 128), 0)
        for quarter in range(4):
            number = ((base + (from_p * own_rows + from_r)) * 4 + quarter).astype(F32)
            table = jnp.where(number == owners, 1.0, 0.0).astype(BF16)
            lanes = slice(quarter * 128, (quarter + 1) * 128)
            r0 = gas[place_p, place_r : place_r + rows, lanes] - jnp.dot(
                table, parts, preferred_element_type=F32
            )
            m = recip[place_p, place_r : place_r + rows, lanes]
            gas[place_p, place_r : place_r + rows, lanes] = r0
            zed[place_p, place_r : place_r + rows, lanes] = m * r0

    far_row = own_rows - 8
    enter(8, 2, first, 0, 0, own_rows)
    enter(8, 3, first, 1, 0, own_rows)
    invert(0, first, own_rows, has_down)
    invert(1, first, own_rows, has_down)
    invert(4, first, own_rows, has_up)
    invert(5, first, own_rows, has_up)
    for p in range(2):
        invert(2 + p, first - 8, 8, has_left)
        invert(2 + p, last, 8, has_right)
    invert(1, first - 8, 8, has_left & has_down)
    invert(1, last, 8, has_right & has_down)
    invert(4, first - 8, 8, has_left & has_up)
    invert(4, last, 8, has_right & has_up)
    for copy in halo_dep:
        copy.wait_recv()
    enter(0, 0, first, 0, 0, own_rows)
    enter(0, 1, first, 1, 0, own_rows)
    enter(1, 4, first, 0, 0, own_rows)
    enter(1, 5, first, 1, 0, own_rows)
    for p in range(2):
        enter(2, 2 + p, first - 8, p, far_row, 8)
        enter(3, 2 + p, last, p, 0, 8)
    enter(4, 1, first - 8, 1, far_row, 8)
    enter(5, 1, last, 1, 0, 8)
    enter(6, 4, first - 8, 0, far_row, 8)
    enter(7, 4, last, 0, 0, 8)

    lane_w = lax.broadcasted_iota(jnp.int32, (8, 512), 1)

    def beside_sum(field, p, row):
        here = field[p, row : row + 8, :]
        ahead = jnp.where(lane_w == 0, 0.0, pltpu.roll(here, 1, 1))
        behind = jnp.where(lane_w == 511, 0.0, pltpu.roll(here, 511, 1))
        result = field[p + 1, row : row + 8, :] + field[p - 1, row : row + 8, :]
        result = result + field[p, row + 1 : row + 9, :]
        result = result + field[p, row - 1 : row + 7, :]
        return result + ahead + behind

    zero = jnp.zeros((8, 512), F32)
    dots = [zero, zero, zero, zero]
    for p in (2, 3, 1, 4):
        inside = p in (2, 3)
        start, stop = (first - 8, last + 8) if inside else (first, last)
        for row in range(start, stop, 8):
            r0 = gas[p, row : row + 8, :]
            u = r0 - beside_sum(zed, p, row)
            w = recip[p, row : row + 8, :] * u
            weighed[p, row : row + 8, :] = w
            if inside and first <= row < last:
                image[p, row : row + 8, :] = u
                z0 = zed[p, row : row + 8, :]
                dots[0] = dots[0] + r0 * z0
                dots[1] = dots[1] + z0 * u
                dots[2] = dots[2] + u * w
    for p in (2, 3):
        for row in range(first, last, 8):
            t = image[p, row : row + 8, :] - beside_sum(weighed, p, row)
            twice[p - 2, row - first : row - first + 8, :] = t
            dots[3] = dots[3] + weighed[p, row : row + 8, :] * t

    lane_one = lax.broadcasted_iota(jnp.int32, (1, 128), 1)
    mine = jnp.zeros((1, 128), F32)
    for k, dot in enumerate(dots):
        fold = jnp.sum(dot, axis=0, keepdims=True)
        fold = fold[:, 0:128] + fold[:, 128:256] + fold[:, 256:384] + fold[:, 384:512]
        fold = fold + pltpu.roll(fold, 64, 1)
        fold = fold + pltpu.roll(fold, 32, 1)
        mine = jnp.where(lane_one // 32 == k, fold, mine)
    row_a[0] = mine

    def share(peers, source, slots, send_sem, recv_sem):
        copies = []
        for k, target in enumerate(peers):
            copies.append(
                pltpu.make_async_remote_copy(
                    src_ref=source.at[0],
                    dst_ref=slots.at[k],
                    send_sem=send_sem.at[k],
                    recv_sem=recv_sem.at[k],
                    device_id=target,
                    device_id_type=MESH,
                )
            )
            copies[-1].start()
        return copies

    sums_a = share(peers_a, row_a, rows_a, send_ra, recv_ra)
    stores = [
        pltpu.make_async_copy(
            gas.at[pl.ds(2, 2), own_span], right_out, store_sem.at[0]
        ),
        pltpu.make_async_copy(
            image.at[pl.ds(2, 2), own_span], image_out, store_sem.at[1]
        ),
        pltpu.make_async_copy(twice, twice_out, store_sem.at[2]),
    ]
    for copy in stores:
        copy.start()

    move.wait()
    targets = [inlet_ref[0, k] for k in range(8)]
    for col in range(8):
        value = jnp.where(targets[0] == col, 1.0, 0.0) * arrived[0]
        for k in range(1, 8):
            value = value + jnp.where(targets[k] == col, 1.0, 0.0) * arrived[k]
        settled[col] = value
        settled[8 + col] = settled[8 + col] * stays[col]
    for row in range(2):
        for part, ref in enumerate((pos_buf, vel_buf)):
            for axis in range(3):
                for col in range(8):
                    ref[axis, row, pl.ds(col, 1), :] = settled[
                        row * 8 + col, pl.ds(3 * part + axis, 1), :
                    ]

    stores += [
        pltpu.make_async_copy(pos_buf, pos_out, store_sem.at[3]),
        pltpu.make_async_copy(vel_buf, vel_out, store_sem.at[4]),
    ]
    for copy in stores[3:]:
        copy.start()
    for copy in halo_a + halo_b + halo_diag + halo_blk + halo_dep:
        copy.wait_send()

    for copy in sums_a:
        copy.wait_recv()
    mine = mine + jnp.sum(rows_a[...], axis=0)
    row_b[0] = mine
    sums_b = share(peers_b, row_b, rows_b, send_rb, recv_rb)
    for copy in sums_a:
        copy.wait_send()
    for copy in stores:
        copy.wait()
    for copy in sums_b:
        copy.wait_recv()
    sums_out[...] = mine + jnp.sum(rows_b[...], axis=0)
    for copy in sums_b:
        copy.wait_send()


def finish(sums, right, image, twice, diag, pos, vel, pos_out, vel_out, press, resid):
    lane = lax.broadcasted_iota(jnp.int32, (1, 128), 1)
    rz, energy, cross, third = (
        jnp.sum(jnp.where(lane // 32 == k, sums[...], 0.0), axis=1, keepdims=True)
        for k in range(4)
    )
    alpha = rz / energy
    renewed = alpha * alpha * cross - rz
    grow = 1.0 + renewed / rz
    second = renewed / (
        grow * grow * energy - 2.0 * grow * alpha * cross + alpha * alpha * third
    )
    near_factor = jnp.broadcast_to(alpha + second * grow, (8, 128))[:, 0:1]
    far_factor = jnp.broadcast_to(second * alpha, (8, 128))[:, 0:1]
    for p in range(2):
        for row in range(0, right.shape[1], 8):
            rows = slice(row, row + 8)
            r0, u = right[p, rows, :], image[p, rows, :]
            m = 1.0 / (6.0 + diag[p, rows, :])
            press[p, rows, :] = m * (near_factor * r0 - far_factor * u)
            resid[p, rows, :] = r0 - near_factor * u + far_factor * twice[p, rows, :]
    pos_out[...] = pos[...]
    vel_out[...] = vel[...]


def on_device(
    depth_z,
    positions,
    velocities,
    contacts,
    exit_flags,
    inlet_slots,
    cell_blocks,
    cell_slots,
    gas_source,
    diagonal,
):
    high = lax.axis_size("height")
    count_a = 2 * depth_z - 1
    count_b = (high // (2 * depth_z)) * lax.axis_size("cols") - 1
    vmem = pl.BlockSpec(memory_space=pltpu.VMEM)
    smem = pl.BlockSpec(memory_space=pltpu.SMEM)
    hbm = pl.BlockSpec(memory_space=pl.ANY)
    dma = pltpu.SemaphoreType.DMA
    own_rows = gas_source.shape[1]
    grid = (6, own_rows + 2 * PAD, gas_source.shape[2])
    field = jax.ShapeDtypeStruct(gas_source.shape, F32)
    state = jax.ShapeDtypeStruct(positions.shape, F32)
    row = jax.ShapeDtypeStruct((1, 128), F32)
    pos, vel, right, image, twice, sums = pl.pallas_call(
        functools.partial(kernel, depth_z),
        out_shape=(state, state, field, field, field, row),
        in_specs=[vmem, vmem, vmem, smem, smem, smem, smem, hbm, hbm],
        out_specs=(hbm, hbm, hbm, hbm, hbm, vmem),
        scratch_shapes=[
            pltpu.VMEM(positions.shape, F32),
            pltpu.VMEM(positions.shape, F32),
            pltpu.VMEM((4, 10, 8, 128), F32),
            pltpu.VMEM((4, 10, 8, 128), F32),
            pltpu.VMEM((4, 48, 1280), BF16),
            pltpu.VMEM((4, 80, 1280), BF16),
            pltpu.VMEM((8, 256, 48), BF16),
            pltpu.VMEM((8, 256, 128), F32),
            pltpu.VMEM((16, 8, 128), F32),
            pltpu.VMEM(grid, F32),
            pltpu.VMEM(grid, F32),
            pltpu.VMEM(grid, F32),
            pltpu.VMEM(grid, F32),
            pltpu.VMEM(grid, F32),
            pltpu.VMEM(grid, F32),
            pltpu.VMEM(gas_source.shape, F32),
            pltpu.VMEM((9, 16, 128), F32),
            pltpu.VMEM((9, 8, 128), F32),
            pltpu.VMEM((8, 8, 128), F32),
            pltpu.VMEM((8, 8, 128), F32),
            pltpu.VMEM((1, 1, 128), F32),
            pltpu.VMEM((count_a, 1, 128), F32),
            pltpu.VMEM((1, 1, 128), F32),
            pltpu.VMEM((count_b, 1, 128), F32),
            dma((2,)),
            dma((5,)),
            pltpu.SemaphoreType.REGULAR((8,)),
            pltpu.SemaphoreType.REGULAR((8,)),
            dma((8,)),
            dma((8,)),
            dma((8,)),
            dma((8,)),
            dma((8,)),
            dma((8,)),
            dma((8,)),
            dma((8,)),
            dma((8,)),
            dma((8,)),
            dma((8,)),
            dma((8,)),
            dma((1,)),
            dma((1,)),
            dma((count_a,)),
            dma((count_a,)),
            dma((count_b,)),
            dma((count_b,)),
        ],
        compiler_params=pltpu.CompilerParams(
            collective_id=0, has_side_effects=True
        ),
    )(
        positions,
        velocities,
        cell_slots,
        jnp.transpose(contacts, (1, 2, 0)),
        exit_flags,
        inlet_slots,
        cell_blocks,
        gas_source,
        diagonal,
    )
    return pl.pallas_call(
        finish,
        out_shape=(state, state, field, field),
        in_specs=[vmem] * 7,
        out_specs=(vmem,) * 4,
    )(sums, right, image, twice, diagonal, pos, vel)


def solution(mesh, depth_z=16):
    in_specs = (
        P(None, "height", "cols", None),
        P(None, "height", "cols", None),
        P(None, "height", "cols"),
        P("height", "cols"),
        P("height", "cols"),
        P("height", "cols"),
        P("height", "cols", None),
        P("height", "cols", None),
        P("height", "cols", None),
    )
    out_specs = (
        P(None, "height", "cols", None),
        P(None, "height", "cols", None),
        P("height", "cols", None),
        P("height", "cols", None),
    )
    return jax.shard_map(
        functools.partial(on_device, depth_z),
        mesh=mesh,
        in_specs=in_specs,
        out_specs=out_specs,
        check_vma=False,
    )
```

```python
import functools

import jax
import jax.numpy as jnp
from jax import lax
from jax.experimental import pallas as pl
from jax.experimental.pallas import tpu as pltpu
from jax.sharding import PartitionSpec as P

MESH = pl.DeviceIdType.MESH
F32 = jnp.float32
BF16 = jnp.bfloat16

spring = 0.05
cutoff_sq = 1.44
damping = 0.5
step_dt = 0.05
gravity = 1.0
deposit_gain = 2.0

PAD = 16
NT_DIMS = (((1,), (1,)), ((), ()))
TN_DIMS = (((0,), (0,)), ((), ()))


def split3(value):
    high = value.astype(BF16).astype(F32)
    rest = value - high
    mid = rest.astype(BF16).astype(F32)
    return high, mid, (rest - mid).astype(BF16).astype(F32)


def kernel(
    depth_z,
    pos_ref,
    vel_ref,
    slots_ref,
    contacts_ref,
    exit_ref,
    inlet_ref,
    blocks_ref,
    gas_ref,
    diag_ref,
    pos_out,
    vel_out,
    right_out,
    image_out,
    twice_out,
    sums_out,
    pos_buf,
    vel_buf,
    tiles_a,
    tiles_b,
    grams,
    pulls,
    owns,
    total,
    settled,
    gas,
    scale,
    recip,
    zed,
    image,
    weighed,
    twice,
    per_tile,
    block_row,
    leaving,
    arrived,
    row_a,
    rows_a,
    row_b,
    rows_b,
    load_sem,
    store_sem,
    known_z,
    known_p,
    send_a,
    recv_a,
    send_b,
    recv_b,
    send_gas,
    recv_gas,
    send_diag,
    recv_diag,
    send_blk,
    recv_blk,
    send_dep,
    recv_dep,
    send_mig,
    recv_mig,
    send_ra,
    recv_ra,
    send_rb,
    recv_rb,
):
    high = lax.axis_size("height")
    wide = lax.axis_size("cols")
    h = lax.axis_index("height")
    c = lax.axis_index("cols")
    up = lax.rem(h + 1, high)
    down = lax.rem(h + high - 1, high)
    right = lax.rem(c + 1, wide)
    left = lax.rem(c + wide - 1, wide)
    goes = (
        (up, c),
        (down, c),
        (h, right),
        (h, left),
        (up, right),
        (up, left),
        (down, right),
        (down, left),
    )
    core = lax.rem(h, 2)
    z = lax.rem(h // 2, depth_z)
    x = h // (2 * depth_z)
    depth_x = high // (2 * depth_z)

    def z_peer(step):
        return (x * depth_z + lax.rem(z + step, depth_z)) * 2 + core

    def x_peer(step):
        return (lax.rem(x + step, depth_x) * depth_z + z) * 2 + core

    def y_peer(step):
        return lax.rem(c + step, wide)

    def far_first(steps, count):
        return sorted(steps, key=lambda step: -min(step, count - step))

    line_z = [z_peer(step) if step else h for step in range(depth_z)]
    line_x = [x_peer(step) if step else h for step in range(depth_x)]
    line_y = [y_peer(step) if step else c for step in range(wide)]
    other_core = 1 - 2 * core
    peers_a = [
        (line_z[step] + flip * other_core, c)
        for step in far_first(range(depth_z), depth_z)
        for flip in range(2)
        if step or flip
    ]
    peers_b = [
        (line_x[step_x], line_y[step_y])
        for step_y in far_first(range(wide), wide)
        for step_x in far_first(range(depth_x), depth_x)
        if step_x or step_y
    ]

    def signal(sem, target):
        pl.semaphore_signal(sem, inc=1, device_id=target, device_id_type=MESH)

    chain_z, chain_p = [], []
    reach = 1
    while reach < depth_z // 2:
        chain_z.append(((z_peer(reach), c), (z_peer(depth_z - reach), c)))
        reach *= 2
    chain_z.append(((h + other_core, c),))
    reach = 1
    while reach < wide // 2:
        chain_p.append(((h, y_peer(reach)), (h, y_peer(wide - reach))))
        reach *= 2
    for _ in range(depth_x // 2):
        chain_p.append(((x_peer(1), c), (x_peer(depth_x - 1), c)))
    stage = [0]

    def spread():
        now = stage[0]
        for chain, sem in ((chain_z, known_z), (chain_p, known_p)):
            if 0 < now <= len(chain):
                pl.semaphore_wait(sem.at[now - 1], len(chain[now - 1]))
        for chain, sem in ((chain_z, known_z), (chain_p, known_p)):
            if now < len(chain):
                for target in chain[now]:
                    signal(sem.at[now], target)
        stage[0] = now + 1

    own_rows = gas_ref.shape[1]
    first, last = PAD, PAD + own_rows
    own_span = pl.ds(first, own_rows)
    load_gas = pltpu.make_async_copy(
        gas_ref, gas.at[pl.ds(2, 2), own_span], load_sem.at[0]
    )
    load_diag = pltpu.make_async_copy(
        diag_ref, scale.at[pl.ds(2, 2), own_span], load_sem.at[1]
    )
    load_gas.start()
    load_diag.start()

    barrier = pltpu.get_barrier_semaphore()
    greeted = goes + (
        (z_peer(1), c),
        (z_peer(depth_z - 1), c),
        (x_peer(1), c),
        (x_peer(depth_x - 1), c),
    )
    for target in greeted:
        signal(barrier, target)

    def send(source, dest, send_sem, recv_sem, k):
        copy = pltpu.make_async_remote_copy(
            src_ref=source,
            dst_ref=dest,
            send_sem=send_sem.at[k],
            recv_sem=recv_sem.at[k],
            device_id=goes[k],
            device_id_type=MESH,
        )
        copy.start()
        return copy

    def send_tiles(tiles, send_sem, recv_sem):
        pairs = (
            (tiles.at[2, pl.ds(1, 8)], tiles.at[0, pl.ds(1, 8)]),
            (tiles.at[1, pl.ds(1, 8)], tiles.at[3, pl.ds(1, 8)]),
            (tiles.at[pl.ds(1, 2), 8], tiles.at[pl.ds(1, 2), 0]),
            (tiles.at[pl.ds(1, 2), 1], tiles.at[pl.ds(1, 2), 9]),
            (tiles.at[2, 8], tiles.at[0, 0]),
            (tiles.at[2, 1], tiles.at[0, 9]),
            (tiles.at[1, 8], tiles.at[3, 0]),
            (tiles.at[1, 1], tiles.at[3, 9]),
        )
        return [
            send(source, dest, send_sem, recv_sem, k)
            for k, (source, dest) in reversed(list(enumerate(pairs)))
        ]

    def send_planes(field, send_sem, recv_sem):
        top, bottom = pl.ds(last - 8, 8), pl.ds(first, 8)
        before, after = pl.ds(first - 8, 8), pl.ds(last, 8)
        mid = pl.ds(2, 2)
        pairs = (
            (field.at[mid, own_span], field.at[pl.ds(0, 2), own_span]),
            (field.at[mid, own_span], field.at[pl.ds(4, 2), own_span]),
            (field.at[mid, top], field.at[mid, before]),
            (field.at[mid, bottom], field.at[mid, after]),
            (field.at[3, top], field.at[1, before]),
            (field.at[3, bottom], field.at[1, after]),
            (field.at[2, top], field.at[4, before]),
            (field.at[2, bottom], field.at[4, after]),
        )
        return [
            send(source, dest, send_sem, recv_sem, k)
            for k, (source, dest) in reversed(list(enumerate(pairs)))
        ]

    comp = lax.broadcasted_iota(jnp.int32, (8, 128), 0)
    lane = lax.broadcasted_iota(jnp.int32, (8, 128), 1)

    for row in range(2):
        for part, ref in enumerate((pos_ref, vel_ref)):
            for axis in range(3):
                value = ref[axis, row]
                for col in range(8):
                    tiles_a[row + 1, col + 1, pl.ds(3 * part + axis, 1), :] = value[
                        col : col + 1
                    ]
        for col in range(8):
            tiles_a[row + 1, col + 1, pl.ds(6, 2), :] = jnp.zeros((2, 128), F32)

    blocks_vec = jnp.full((8, 128), -1, jnp.int32)
    for tile in range(16):
        blocks_vec = jnp.where(
            (lane < 48) & (lax.rem(lane, 16) == tile),
            blocks_ref[tile // 8, tile % 8],
            blocks_vec,
        )
    block_row[8] = blocks_vec.astype(F32)

    span = (2.0 * spring / cutoff_sq) ** 0.5

    def features(tiles, row, col, edge):
        tile = tiles[row, col]
        if edge is not None:
            tile = jnp.where(edge, tile, 0.0)
        shift_x = (col - 4.5) if isinstance(col, int) else (col.astype(F32) - 4.5)
        shift_z = (row - 1.5) if isinstance(row, int) else (row.astype(F32) - 1.5)
        shift = jnp.where(comp == 0, shift_x, jnp.where(comp == 2, shift_z, 0.0))
        at = tile + shift
        speed = pltpu.roll(tile, 5, 0)
        moving = at - damping * speed
        unit = jnp.where(comp < 3, span * at, 0.0)
        half = -0.5 * jnp.sum(unit * unit, axis=0, keepdims=True)
        gram = jnp.where(comp == 3, half, jnp.where(comp == 4, 1.0, unit))
        g_high, g_mid, g_low = split3(gram)
        lanes = pl.ds(col * 128, 128)
        if not isinstance(col, int):
            lanes = pl.ds(pl.multiple_of(col * 128, 128), 128)
        grams[row, :, lanes] = jnp.concatenate(
            [g_high, g_mid, g_high, g_mid, g_low, g_high], axis=0
        ).astype(BF16)
        pull = jnp.where(comp < 3, moving, jnp.where(comp == 3, 1.0, 0.0))
        pull = jnp.where(comp < 4, pull, pltpu.roll(pull, 4, 0))
        products = [
            pull * jnp.where(comp < 4, unit[0:1], unit[1:2]),
            pull * jnp.where(comp < 4, unit[2:3], half),
            jnp.where(comp < 4, pull, 0.0),
        ]
        parts = [split3(product) for product in products]
        pulls[row, :, lanes] = jnp.concatenate(
            [part[level] for level in range(3) for part in parts]
            + [jnp.zeros((8, 128), F32)],
            axis=0,
        ).astype(BF16)
        return unit, half

    def own_features(tiles, row, col):
        unit, half = features(tiles, row + 1, col + 1, None)
        gram = jnp.where(comp == 4, half + spring, jnp.where(comp == 3, 1.0, unit))
        f_high, f_mid, f_low = split3(gram)
        block = jnp.concatenate([f_high, f_high, f_mid, f_mid, f_high, f_low], axis=0)
        owns[col, pl.ds(row * 128, 128), :] = jnp.transpose(
            jnp.concatenate([block, jnp.zeros((80, 128), F32)], axis=0)
        )[:, :48].astype(BF16)

    def gather(jobs):
        steps = []
        for rows, col, pieces, fresh in jobs:
            blocks = [
                (other, step)
                for other, start, count in pieces
                for step in range(start, start + count)
            ]
            for at in range(0, len(blocks), 6):
                last = at + 6 >= len(blocks)
                steps.append((rows, col, blocks[at : at + 6], at == 0, last, fresh))

        def stack(table, col, group):
            parts = []
            for other, step in group:
                begin = (col + step) * 128
                if not isinstance(col, int):
                    begin = pl.multiple_of(begin, 128)
                parts.append(table[other, :, pl.ds(begin, 128)])
            return jnp.concatenate(parts, 1)

        def score(rows, col, group, *_):
            mine = owns[col, rows[0] * 128 : (rows[-1] + 1) * 128, :]
            return jnp.dot(mine, stack(grams, col, group), preferred_element_type=F32)

        ready = [score(*step) for step in steps[:1]]
        result = None
        for n, (rows, col, group, begins, ends, fresh) in enumerate(steps):
            if n + 1 < len(steps):
                ready.append(score(*steps[n + 1]))
            scores = ready.pop(0)
            kept = []
            for k, row in enumerate(rows):
                parts = []
                for m, (other, step) in enumerate(group):
                    flag = contacts_ref[row, col, (other - row) * 3 + step].astype(F32)
                    here = scores[k * 128 : (k + 1) * 128, m * 128 : (m + 1) * 128]
                    parts.append(jnp.where(here > 0.0, flag, 0.0).astype(BF16))
                kept.append(jnp.concatenate(parts, 1))
            part = lax.dot_general(
                jnp.concatenate(kept, 0),
                stack(pulls, col, group),
                NT_DIMS,
                preferred_element_type=F32,
            )
            result = part if begins else result + part
            if ends:
                span_p = slice(rows[0] * 128, (rows[-1] + 1) * 128)
                if not fresh:
                    result = result + total[col, span_p, 0:80]
                total[col, span_p, 0:80] = result

    def own_tiles(tiles):
        def make(index, carry):
            own_features(tiles, 0, index)
            own_features(tiles, 1, index)
            return carry

        lax.fori_loop(0, 8, make, 0, unroll=2)

    def near():
        both = (0, 1)
        gather(
            [
                (both, 0, ((1, 1, 2), (2, 1, 2)), True),
                (both, 7, ((1, 0, 2), (2, 0, 2)), True),
            ]
        )

        def inner(index, carry):
            cols = [index * 2 + 1 + k for k in range(2)]
            gather([(both, col, ((1, 0, 3), (2, 0, 3)), True) for col in cols])
            return carry

        lax.fori_loop(0, 6 // 2, inner, 0)

    has_up, has_down = h < high - 1, h > 0
    has_right, has_left = c < wide - 1, c > 0

    def far(tiles):
        def beside(row, carry):
            features(tiles, row, 0, has_left)
            features(tiles, row, 9, has_right)
            return carry

        lax.fori_loop(1, 3, beside, 0)
        features(tiles, 0, 0, has_left & has_down)
        features(tiles, 0, 9, has_right & has_down)
        features(tiles, 3, 0, has_left & has_up)
        features(tiles, 3, 9, has_right & has_up)

        def above(col, carry):
            features(tiles, 0, col, has_down)
            features(tiles, 3, col, has_up)
            return carry

        lax.fori_loop(1, 9, above, 0, unroll=2)

        def inner(index, carry):
            jobs = []
            for k in range(2):
                jobs.append(((0,), index * 2 + 1 + k, ((0, 0, 3),), False))
                jobs.append(((1,), index * 2 + 1 + k, ((3, 0, 3),), False))
            gather(jobs)
            return carry

        lax.fori_loop(0, 6 // 2, inner, 0)
        jobs = []
        for row in range(2):
            jobs.append(((row,), 0, ((3 * row, 0, 3), (1, 0, 1), (2, 0, 1)), False))
            jobs.append(((row,), 7, ((3 * row, 0, 3), (1, 2, 1), (2, 2, 1)), False))
        gather(jobs)

    def advanced(tiles, row, col):
        tile = tiles[row + 1, col + 1]
        sums = jnp.transpose(total[col, pl.ds(row * 128, 128), :])
        sums = sums[0:24] + sums[24:48] + sums[48:72]
        shift = jnp.where(
            comp == 0,
            col.astype(F32) - 3.5,
            jnp.where(comp == 2, row - 0.5, 0.0),
        )
        at = tile + shift
        moving = at - damping * pltpu.roll(tile, 5, 0)
        unit = jnp.where(comp < 3, span * at, 0.0)
        half = -0.5 * jnp.sum(unit * unit, axis=0, keepdims=True)
        pulled = (
            sums[0:8] * jnp.where(comp < 4, unit[0:1], unit[1:2])
            + sums[8:16] * jnp.where(comp < 4, unit[2:3], 1.0)
            + sums[16:24] * (half + spring)
        )
        pulled = pulled + pltpu.roll(pulled, 4, 0)
        force = pltpu.roll(moving * pulled[3:4] - pulled, 3, 0)
        speeds = tile + step_dt * force - jnp.where(comp == 5, step_dt * gravity, 0.0)
        places = tile + step_dt * pltpu.roll(speeds, 5, 0)
        return jnp.where(comp < 3, places, jnp.where(comp < 6, speeds, 0.0))

    pl.semaphore_wait(barrier, len(greeted))
    spread()

    halo_a = send_tiles(tiles_a, send_a, recv_a)
    load_gas.wait()
    load_diag.wait()
    halo_gas = send_planes(gas, send_gas, recv_gas)
    halo_blk = [
        send(block_row.at[8], block_row.at[k], send_blk, recv_blk, k) for k in range(8)
    ]
    own_tiles(tiles_a)
    near()
    for copy in halo_a:
        copy.wait_recv()
    spread()
    far(tiles_a)
    spread()

    def first_step(col, carry):
        tiles_b[1, col + 1] = advanced(tiles_a, 0, col)
        tiles_b[2, col + 1] = advanced(tiles_a, 1, col)
        return carry

    lax.fori_loop(0, 8, first_step, 0, unroll=4)
    halo_b = send_tiles(tiles_b, send_b, recv_b)
    halo_diag = send_planes(scale, send_diag, recv_diag)
    own_tiles(tiles_b)
    near()
    spread()

    def invert(place_p, place_r, rows, valid):
        for row in range(place_r, place_r + rows, 8):
            m = 1.0 / (6.0 + scale[place_p, row : row + 8, :])
            if valid is not None:
                m = jnp.where(valid, m, 0.0)
            recip[place_p, row : row + 8, :] = m

    invert(2, first, own_rows, None)
    invert(3, first, own_rows, None)
    for copy in halo_b:
        copy.wait_recv()
    far(tiles_b)
    spread()

    count_row = lax.broadcasted_iota(jnp.int32, (128, 128), 0)

    def second_step(col, carry):
        for row in range(2):
            tile = advanced(tiles_b, row, col)
            settled[row * 8 + col] = tile
            lift = deposit_gain * tile[5:6]
            l_high, l_mid, l_low = split3(lift)
            rows = jnp.where(
                comp == 0,
                l_high,
                jnp.where(comp == 1, l_mid, jnp.where(comp == 2, l_low, 0.0)),
            )
            slot = slots_ref[row, pl.ds(col, 1), :]
            table = jnp.where(count_row == slot, 1.0, 0.0).astype(BF16)
            placed = lax.dot_general(
                jnp.concatenate([rows, jnp.zeros((8, 128), F32)], axis=0).astype(BF16),
                table,
                NT_DIMS,
                preferred_element_type=F32,
            )
            per_tile[8, pl.ds(row * 8 + col, 1), :] = jnp.sum(
                placed[0:8], axis=0, keepdims=True
            )
        return carry

    lax.fori_loop(0, 8, second_step, 0, unroll=4)
    halo_dep = [
        send(per_tile.at[8], per_tile.at[k], send_dep, recv_dep, k)
        for k in reversed(range(8))
    ]

    rank = jnp.int32(0)
    picks = [[None] * 8 for _ in range(8)]
    stays = []
    for col in range(8):
        flag = exit_ref[1, col]
        for k in range(8):
            picks[k][col] = jnp.where(rank == k, flag, 0).astype(F32)
        stays.append((1 - flag).astype(F32))
        rank = rank + flag
    for k in range(8):
        value = picks[k][0] * settled[8]
        for col in range(1, 8):
            value = value + picks[k][col] * settled[8 + col]
        leaving[k] = value
    move = pltpu.make_async_remote_copy(
        src_ref=leaving,
        dst_ref=arrived,
        send_sem=send_mig.at[0],
        recv_sem=recv_mig.at[0],
        device_id=(up, c),
        device_id_type=MESH,
    )
    move.start()

    for copy in halo_gas:
        copy.wait_recv()
    for copy in halo_diag:
        copy.wait_recv()
    for copy in halo_gas:
        copy.wait_send()
    for copy in halo_blk:
        copy.wait_recv()

    def enter(source, place_p, place_r, from_p, from_r, rows):
        parts = jnp.concatenate(
            list(split3(per_tile[source])) + [jnp.zeros((80, 128), F32)], axis=0
        ).astype(BF16)
        owners = block_row[source][0:1]
        base = lax.broadcasted_iota(jnp.int32, (rows, 128), 0)
        for quarter in range(4):
            number = ((base + (from_p * own_rows + from_r)) * 4 + quarter).astype(F32)
            table = jnp.where(number == owners, 1.0, 0.0).astype(BF16)
            lanes = slice(quarter * 128, (quarter + 1) * 128)
            r0 = gas[place_p, place_r : place_r + rows, lanes] - jnp.dot(
                table, parts, preferred_element_type=F32
            )
            m = recip[place_p, place_r : place_r + rows, lanes]
            gas[place_p, place_r : place_r + rows, lanes] = r0
            zed[place_p, place_r : place_r + rows, lanes] = m * r0

    far_row = own_rows - 8
    enter(8, 2, first, 0, 0, own_rows)
    enter(8, 3, first, 1, 0, own_rows)
    invert(0, first, own_rows, has_down)
    invert(1, first, own_rows, has_down)
    invert(4, first, own_rows, has_up)
    invert(5, first, own_rows, has_up)
    for p in range(2):
        invert(2 + p, first - 8, 8, has_left)
        invert(2 + p, last, 8, has_right)
    invert(1, first - 8, 8, has_left & has_down)
    invert(1, last, 8, has_right & has_down)
    invert(4, first - 8, 8, has_left & has_up)
    invert(4, last, 8, has_right & has_up)
    for copy in halo_dep:
        copy.wait_recv()
    enter(0, 0, first, 0, 0, own_rows)
    enter(0, 1, first, 1, 0, own_rows)
    enter(1, 4, first, 0, 0, own_rows)
    enter(1, 5, first, 1, 0, own_rows)
    for p in range(2):
        enter(2, 2 + p, first - 8, p, far_row, 8)
        enter(3, 2 + p, last, p, 0, 8)
    enter(4, 1, first - 8, 1, far_row, 8)
    enter(5, 1, last, 1, 0, 8)
    enter(6, 4, first - 8, 0, far_row, 8)
    enter(7, 4, last, 0, 0, 8)

    lane_w = lax.broadcasted_iota(jnp.int32, (8, 512), 1)

    def beside_sum(field, p, row):
        here = field[p, row : row + 8, :]
        ahead = jnp.where(lane_w == 0, 0.0, pltpu.roll(here, 1, 1))
        behind = jnp.where(lane_w == 511, 0.0, pltpu.roll(here, 511, 1))
        result = field[p + 1, row : row + 8, :] + field[p - 1, row : row + 8, :]
        result = result + field[p, row + 1 : row + 9, :]
        result = result + field[p, row - 1 : row + 7, :]
        return result + ahead + behind

    zero = jnp.zeros((8, 512), F32)
    dots = [zero, zero, zero, zero]
    for p in (2, 3, 1, 4):
        inside = p in (2, 3)
        start, stop = (first - 8, last + 8) if inside else (first, last)
        for row in range(start, stop, 8):
            r0 = gas[p, row : row + 8, :]
            u = r0 - beside_sum(zed, p, row)
            w = recip[p, row : row + 8, :] * u
            weighed[p, row : row + 8, :] = w
            if inside and first <= row < last:
                image[p, row : row + 8, :] = u
                z0 = zed[p, row : row + 8, :]
                dots[0] = dots[0] + r0 * z0
                dots[1] = dots[1] + z0 * u
                dots[2] = dots[2] + u * w
    for p in (2, 3):
        for row in range(first, last, 8):
            t = image[p, row : row + 8, :] - beside_sum(weighed, p, row)
            twice[p - 2, row - first : row - first + 8, :] = t
            dots[3] = dots[3] + weighed[p, row : row + 8, :] * t

    lane_one = lax.broadcasted_iota(jnp.int32, (1, 128), 1)
    mine = jnp.zeros((1, 128), F32)
    for k, dot in enumerate(dots):
        fold = jnp.sum(dot, axis=0, keepdims=True)
        fold = fold[:, 0:128] + fold[:, 128:256] + fold[:, 256:384] + fold[:, 384:512]
        fold = fold + pltpu.roll(fold, 64, 1)
        fold = fold + pltpu.roll(fold, 32, 1)
        mine = jnp.where(lane_one // 32 == k, fold, mine)
    row_a[0] = mine

    def share(peers, source, slots, send_sem, recv_sem):
        copies = []
        for k, target in enumerate(peers):
            copies.append(
                pltpu.make_async_remote_copy(
                    src_ref=source.at[0],
                    dst_ref=slots.at[k],
                    send_sem=send_sem.at[k],
                    recv_sem=recv_sem.at[k],
                    device_id=target,
                    device_id_type=MESH,
                )
            )
            copies[-1].start()
        return copies

    sums_a = share(peers_a, row_a, rows_a, send_ra, recv_ra)
    stores = [
        pltpu.make_async_copy(
            gas.at[pl.ds(2, 2), own_span], right_out, store_sem.at[0]
        ),
        pltpu.make_async_copy(
            image.at[pl.ds(2, 2), own_span], image_out, store_sem.at[1]
        ),
        pltpu.make_async_copy(twice, twice_out, store_sem.at[2]),
    ]
    for copy in stores:
        copy.start()

    move.wait()
    targets = [inlet_ref[0, k] for k in range(8)]
    for col in range(8):
        value = jnp.where(targets[0] == col, 1.0, 0.0) * arrived[0]
        for k in range(1, 8):
            value = value + jnp.where(targets[k] == col, 1.0, 0.0) * arrived[k]
        settled[col] = value
        settled[8 + col] = settled[8 + col] * stays[col]
    for row in range(2):
        for part, ref in enumerate((pos_buf, vel_buf)):
            for axis in range(3):
                for col in range(8):
                    ref[axis, row, pl.ds(col, 1), :] = settled[
                        row * 8 + col, pl.ds(3 * part + axis, 1), :
                    ]

    stores += [
        pltpu.make_async_copy(pos_buf, pos_out, store_sem.at[3]),
        pltpu.make_async_copy(vel_buf, vel_out, store_sem.at[4]),
    ]
    for copy in stores[3:]:
        copy.start()
    for copy in halo_a + halo_b + halo_diag + halo_blk + halo_dep:
        copy.wait_send()

    for copy in sums_a:
        copy.wait_recv()
    mine = mine + jnp.sum(rows_a[...], axis=0)
    row_b[0] = mine
    sums_b = share(peers_b, row_b, rows_b, send_rb, recv_rb)
    for copy in sums_a:
        copy.wait_send()
    for copy in stores:
        copy.wait()
    for copy in sums_b:
        copy.wait_recv()
    sums_out[...] = mine + jnp.sum(rows_b[...], axis=0)
    for copy in sums_b:
        copy.wait_send()


def finish(
    sums_in,
    right_in,
    image_in,
    twice_in,
    diag_in,
    pos_in,
    vel_in,
    pos_out,
    vel_out,
    press_out,
    resid_out,
    sums,
    right,
    image,
    twice,
    diag,
    state,
    press,
    resid,
    sem,
    load_sem,
    store_sem,
):
    first = [
        pltpu.make_async_copy(sums_in, sums, sem.at[0]),
        pltpu.make_async_copy(pos_in, state.at[0], sem.at[1]),
        pltpu.make_async_copy(vel_in, state.at[1], sem.at[2]),
    ]
    first[0].start()
    loads = [
        [
            pltpu.make_async_copy(source.at[p], dest.at[p], load_sem.at[p, k])
            for k, (source, dest) in enumerate(
                ((right_in, right), (image_in, image), (twice_in, twice), (diag_in, diag))
            )
        ]
        for p in range(2)
    ]
    for copy in loads[0] + loads[1] + first[1:]:
        copy.start()
    first[0].wait()
    lane = lax.broadcasted_iota(jnp.int32, (1, 128), 1)
    rz, energy, cross, third = (
        jnp.sum(jnp.where(lane // 32 == k, sums[...], 0.0), axis=1, keepdims=True)
        for k in range(4)
    )
    alpha = rz / energy
    renewed = alpha * alpha * cross - rz
    grow = 1.0 + renewed / rz
    second = renewed / (
        grow * grow * energy - 2.0 * grow * alpha * cross + alpha * alpha * third
    )
    near_factor = jnp.broadcast_to(alpha + second * grow, (8, 128))[:, 0:1]
    far_factor = jnp.broadcast_to(second * alpha, (8, 128))[:, 0:1]
    stores = []
    for p in range(2):
        for copy in loads[p]:
            copy.wait()
        for row in range(0, right.shape[1], 8):
            rows = slice(row, row + 8)
            r0, u = right[p, rows, :], image[p, rows, :]
            m = 1.0 / (6.0 + diag[p, rows, :])
            press[p, rows, :] = m * (near_factor * r0 - far_factor * u)
            resid[p, rows, :] = r0 - near_factor * u + far_factor * twice[p, rows, :]
        for k, (source, dest) in enumerate(((press, press_out), (resid, resid_out))):
            stores.append(
                pltpu.make_async_copy(source.at[p], dest.at[p], store_sem.at[p, k])
            )
            stores[-1].start()
    for k, dest in enumerate((pos_out, vel_out)):
        first[1 + k].wait()
        stores.append(pltpu.make_async_copy(state.at[k], dest, store_sem.at[2, k]))
        stores[-1].start()
    for copy in stores:
        copy.wait()


def on_device(
    depth_z,
    positions,
    velocities,
    contacts,
    exit_flags,
    inlet_slots,
    cell_blocks,
    cell_slots,
    gas_source,
    diagonal,
):
    high = lax.axis_size("height")
    count_a = 2 * depth_z - 1
    count_b = (high // (2 * depth_z)) * lax.axis_size("cols") - 1
    vmem = pl.BlockSpec(memory_space=pltpu.VMEM)
    smem = pl.BlockSpec(memory_space=pltpu.SMEM)
    hbm = pl.BlockSpec(memory_space=pl.ANY)
    dma = pltpu.SemaphoreType.DMA
    own_rows = gas_source.shape[1]
    grid = (6, own_rows + 2 * PAD, gas_source.shape[2])
    field = jax.ShapeDtypeStruct(gas_source.shape, F32)
    state = jax.ShapeDtypeStruct(positions.shape, F32)
    row = jax.ShapeDtypeStruct((1, 128), F32)
    pos, vel, right, image, twice, sums = pl.pallas_call(
        functools.partial(kernel, depth_z),
        out_shape=(state, state, field, field, field, row),
        in_specs=[vmem, vmem, vmem, smem, smem, smem, smem, hbm, hbm],
        out_specs=(hbm, hbm, hbm, hbm, hbm, vmem),
        scratch_shapes=[
            pltpu.VMEM(positions.shape, F32),
            pltpu.VMEM(positions.shape, F32),
            pltpu.VMEM((4, 10, 8, 128), F32),
            pltpu.VMEM((4, 10, 8, 128), F32),
            pltpu.VMEM((4, 48, 1280), BF16),
            pltpu.VMEM((4, 80, 1280), BF16),
            pltpu.VMEM((8, 256, 48), BF16),
            pltpu.VMEM((8, 256, 128), F32),
            pltpu.VMEM((16, 8, 128), F32),
            pltpu.VMEM(grid, F32),
            pltpu.VMEM(grid, F32),
            pltpu.VMEM(grid, F32),
            pltpu.VMEM(grid, F32),
            pltpu.VMEM(grid, F32),
            pltpu.VMEM(grid, F32),
            pltpu.VMEM(gas_source.shape, F32),
            pltpu.VMEM((9, 16, 128), F32),
            pltpu.VMEM((9, 8, 128), F32),
            pltpu.VMEM((8, 8, 128), F32),
            pltpu.VMEM((8, 8, 128), F32),
            pltpu.VMEM((1, 1, 128), F32),
            pltpu.VMEM((count_a, 1, 128), F32),
            pltpu.VMEM((1, 1, 128), F32),
            pltpu.VMEM((count_b, 1, 128), F32),
            dma((2,)),
            dma((5,)),
            pltpu.SemaphoreType.REGULAR((8,)),
            pltpu.SemaphoreType.REGULAR((8,)),
            dma((8,)),
            dma((8,)),
            dma((8,)),
            dma((8,)),
            dma((8,)),
            dma((8,)),
            dma((8,)),
            dma((8,)),
            dma((8,)),
            dma((8,)),
            dma((8,)),
            dma((8,)),
            dma((1,)),
            dma((1,)),
            dma((count_a,)),
            dma((count_a,)),
            dma((count_b,)),
            dma((count_b,)),
        ],
        compiler_params=pltpu.CompilerParams(
            collective_id=0, has_side_effects=True
        ),
    )(
        positions,
        velocities,
        cell_slots,
        jnp.transpose(contacts, (1, 2, 0)),
        exit_flags,
        inlet_slots,
        cell_blocks,
        gas_source,
        diagonal,
    )
    return pl.pallas_call(
        finish,
        out_shape=(state, state, field, field),
        in_specs=[hbm] * 7,
        out_specs=(hbm,) * 4,
        scratch_shapes=[pltpu.VMEM((1, 128), F32)]
        + [pltpu.VMEM(gas_source.shape, F32)] * 4
        + [pltpu.VMEM((2,) + positions.shape, F32)]
        + [pltpu.VMEM(gas_source.shape, F32)] * 2
        + [dma((3,)), dma((2, 4)), dma((3, 2))],
    )(sums, right, image, twice, diagonal, pos, vel)


def solution(mesh, depth_z=16):
    in_specs = (
        P(None, "height", "cols", None),
        P(None, "height", "cols", None),
        P(None, "height", "cols"),
        P("height", "cols"),
        P("height", "cols"),
        P("height", "cols"),
        P("height", "cols", None),
        P("height", "cols", None),
        P("height", "cols", None),
    )
    out_specs = (
        P(None, "height", "cols", None),
        P(None, "height", "cols", None),
        P("height", "cols", None),
        P("height", "cols", None),
    )
    return jax.shard_map(
        functools.partial(on_device, depth_z),
        mesh=mesh,
        in_specs=in_specs,
        out_specs=out_specs,
        check_vma=False,
    )
```
